256 devices in a mesh: tm: 32 (over z, y_hi, core), plane: 8 (over x, y_lo).
Axes of the slice: x: 4, y: 4 (y_hi: 2, y_lo: 2; y = y_hi * 2 + y_lo), z: 8, core: 2. Of those that a mesh axis runs over, the one named last changes fastest.
Arguments:
- frames: bfloat16 [64, 8, 512, 1024], P('tm', 'plane'), may hold values from -6 to 6
- template: bfloat16 [32, 8, 128, 128], P('tm', 'plane'), may hold values from -6 to 6
- shift_codes: int32 [64, 2, 32], P('tm'), may hold values from -128 to 127
Outputs:
- correlation: float32 [64, 32, 256], P('tm', 'plane')
- new_template: float32 [32, 8, 128, 128], P('tm', 'plane')
The draws below stay inside these ranges and needn't reach their ends.
Inputs may be any that keep to these rules, and one draw needn't show every extreme that they name: shift_codes is 16 times the shift in pixels, its integer part at most 8 pixels either way; every plane of a volume shares it.
All inputs are finite; a program needn't handle non-finite values.
Results may differ from the reference program's by a relative error of at most 0.0065.
Values may be sent and summed in bfloat16 or wider, within the bound.
A program may use at most 128 MiB of HBM per device.

```python
import math
import jax
import jax.numpy as jnp
from jax import lax

BLOCK = 128
IMG_W = 1024
IMG_H = 512
SHIFT = 8
WIN = 16
TAPS = 8
SUB = 16
VOLS = 64
PLANES = 8
BX = 8
BY = 4
BLOCKS = 32


def touch_ends(entries, stream_key, smallest, top_value):
    extent = entries.shape
    index_at = [jax.random.randint(jax.random.fold_in(stream_key, axis), (), 0, extent[axis]) for axis in range(len(extent))]
    entries = entries.at[tuple(index_at)].set(smallest)
    longest = extent.index(max(extent))
    index_at[longest] = (index_at[longest] + 1) % extent[longest]
    return entries.at[tuple(index_at)].set(top_value)


def levels(stream_key, shape, cuts, smallest, high):
    def one(axis_at, blocks):
        steps = jax.random.uniform(jax.random.fold_in(jax.random.fold_in(stream_key, 6), axis_at), (blocks,), jnp.float32, smallest / len(cuts), high / len(cuts))
        return jnp.repeat(jnp.exp(steps), shape[axis_at] // blocks).reshape((-1,) + (1,) * (len(shape) - axis_at - 1))

    level = one(*cuts[0])
    for cut in cuts[1:]:
        level = level * one(*cut)
    return level


def gaussian(stream_key, extent, spread, reach, cuts=(), kind=jnp.bfloat16):
    values = jax.random.normal(stream_key, extent, jnp.float32) * spread
    if len(cuts) > 0:
        values = levels(stream_key, extent, cuts, -0.22, 0.18) * values
    return jnp.clip(values, min=-reach, max=reach).astype(kind)


def setup_inputs(seed: int = 0) -> dict:
    key_of = jax.random.split(jax.random.key(seed), 4)
    return {
        "frames": gaussian(key_of[0], (VOLS, PLANES, IMG_H, IMG_W), 1.0, 6.0, ((0, 32), (1, 8))),
        "template": gaussian(key_of[1], (BLOCKS, PLANES, BLOCK, BLOCK), 1.0, 6.0, ((0, 32), (1, 8))),
        "shift_codes": touch_ends(jax.random.randint(key_of[2], (VOLS, 2, BLOCKS), -SHIFT * SUB, SHIFT * SUB), jax.random.fold_in(key_of[2], 1), -SHIFT * SUB, (SHIFT * SUB) - 1).astype(jnp.int32),
    }


full_turn = 2.0 * math.pi

def dft_tables(block_size):
    positions = jnp.arange(block_size, dtype=jnp.int32)
    product = jnp.mod(positions[:, None] * positions[None, :], block_size)
    angles = product.astype(jnp.float32) * (full_turn / block_size)
    return (jnp.cos(angles).astype(jnp.bfloat16), (-jnp.sin(angles)).astype(jnp.bfloat16))

def spectrum(blocks, cosine_table, sine_table):
    highest = lax.Precision.HIGHEST
    blocks_wide = blocks.astype(jnp.float32)
    cos_wide = cosine_table.astype(jnp.float32)
    sin_wide = sine_table.astype(jnp.float32)
    row_real = jnp.einsum('...rc,ck->...rk', blocks_wide, cos_wide, precision=highest)
    row_imag = jnp.einsum('...rc,ck->...rk', blocks_wide, sin_wide, precision=highest)
    row_real = lax.optimization_barrier(row_real.astype(jnp.bfloat16)).astype(jnp.float32)
    row_imag = lax.optimization_barrier(row_imag.astype(jnp.bfloat16)).astype(jnp.float32)
    real_part = jnp.einsum('kr,...rl->...kl', cos_wide, row_real, precision=highest) - jnp.einsum('kr,...rl->...kl', sin_wide, row_imag, precision=highest)
    imag_part = jnp.einsum('kr,...rl->...kl', cos_wide, row_imag, precision=highest) + jnp.einsum('kr,...rl->...kl', sin_wide, row_real, precision=highest)
    return (real_part, imag_part)

def normalized_cross(frame_real, frame_imag, temp_real, temp_imag):
    temp_real = temp_real.astype(jnp.float32)
    temp_imag = temp_imag.astype(jnp.float32)
    cross_real = frame_real * temp_real + frame_imag * temp_imag
    cross_imag = frame_imag * temp_real - frame_real * temp_imag
    magnitude = jnp.sqrt(cross_real * cross_real + cross_imag * cross_imag)
    mean_mag = lax.optimization_barrier(jnp.mean(magnitude, axis=(-2, -1), keepdims=True)) + 1e-06
    return (cross_real / (magnitude + mean_mag), cross_imag / (magnitude + mean_mag))

def window_tables(shifts, block_size, window):
    offsets = jnp.arange(window, dtype=jnp.int32) - window // 2
    lags = jnp.mod(shifts[:, None] + offsets[None, :], block_size)
    positions = jnp.arange(block_size, dtype=jnp.int32)
    product = jnp.mod(positions[None, :, None] * lags[:, None, :], block_size)
    angles = product.astype(jnp.float32) * (full_turn / block_size)
    return (jnp.cos(angles), jnp.sin(angles))

def windows(norm_real, norm_imag, shift_rows, shift_cols, block_size, window):
    highest = lax.Precision.HIGHEST
    row_cos, row_sin = window_tables(shift_rows, block_size, window)
    col_cos, col_sin = window_tables(shift_cols, block_size, window)
    prod_real = jnp.einsum('nkl,nlc->nkc', norm_real, col_cos, precision=highest) - jnp.einsum('nkl,nlc->nkc', norm_imag, col_sin, precision=highest)
    prod_imag = jnp.einsum('nkl,nlc->nkc', norm_real, col_sin, precision=highest) + jnp.einsum('nkl,nlc->nkc', norm_imag, col_cos, precision=highest)
    result = jnp.einsum('nka,nkc->nac', row_cos, prod_real, precision=highest) - jnp.einsum('nka,nkc->nac', row_sin, prod_imag, precision=highest)
    result = result * (1.0 / block_size)
    return result.reshape(result.shape[0], window * window)

def tap_table(fractions, taps, steps):
    offsets = jnp.arange(taps, dtype=jnp.float32) - (taps // 2 - 1)
    spots = offsets - fractions[..., None].astype(jnp.float32) / steps
    raw_taps = jnp.sinc(spots) * jnp.sinc(spots / (taps // 2))
    return raw_taps / lax.optimization_barrier(jnp.sum(raw_taps, axis=-1, keepdims=True))

def warp_block(padded, row_start, col_start, tap_rows, tap_cols, block_size, taps):
    span = block_size + taps - 1
    region = lax.dynamic_slice(padded, (row_start, col_start), (span, span)).astype(jnp.float32)
    across = jnp.zeros((span, block_size), jnp.float32)
    for tap_index in range(taps):
        across = across + tap_cols[tap_index] * region[:, tap_index:tap_index + block_size]
    result = jnp.zeros((block_size, block_size), jnp.float32)
    for tap_index in range(taps):
        result = result + tap_rows[tap_index] * across[tap_index:tap_index + block_size, :]
    return result

def reference(frames, template, shift_codes):
    cosine_table, sine_table = dft_tables(BLOCK)
    temp_real, temp_imag = spectrum(template, cosine_table, sine_table)
    temp_real = lax.optimization_barrier(temp_real.astype(jnp.bfloat16))
    temp_imag = lax.optimization_barrier(temp_imag.astype(jnp.bfloat16))
    shifts = jnp.floor_divide(shift_codes, SUB).astype(jnp.int32)
    fractions = jnp.mod(shift_codes, SUB).astype(jnp.int32)
    margin = SHIFT + TAPS
    block_ids = jnp.arange(BLOCKS, dtype=jnp.int32)
    block_rows = block_ids // BX * BLOCK
    block_cols = block_ids % BX * BLOCK
    warper = jax.vmap(jax.vmap(partial_warp(BLOCK, TAPS), in_axes=(None, 0, 0, 0, 0)), in_axes=(0, None, None, None, None))

    def one_volume(summed, inputs):
        volume, vol_shift, vol_frac = inputs
        blocks = volume.reshape(PLANES, BY, BLOCK, BX, BLOCK).transpose(1, 3, 0, 2, 4)
        blocks = blocks.reshape(BLOCKS, PLANES, BLOCK, BLOCK)
        frame_real, frame_imag = spectrum(blocks, cosine_table, sine_table)
        norm_real, norm_imag = normalized_cross(frame_real, frame_imag, temp_real, temp_imag)
        shift_rows = jnp.broadcast_to(vol_shift[0][:, None], (BLOCKS, PLANES)).reshape(-1)
        shift_cols = jnp.broadcast_to(vol_shift[1][:, None], (BLOCKS, PLANES)).reshape(-1)
        window_out = windows(norm_real.reshape(-1, BLOCK, BLOCK), norm_imag.reshape(-1, BLOCK, BLOCK), shift_rows, shift_cols, BLOCK, WIN)
        window_out = lax.optimization_barrier(jnp.sum(window_out.reshape(BLOCKS, PLANES, WIN * WIN), axis=1))
        tap_rows = tap_table(vol_frac[0], TAPS, SUB)
        tap_cols = tap_table(vol_frac[1], TAPS, SUB)
        padded = jnp.pad(volume, ((0, 0), (margin, margin), (margin, margin)))
        row_start = (block_rows + margin + vol_shift[0] - (TAPS // 2 - 1)).astype(jnp.int32)
        col_start = (block_cols + margin + vol_shift[1] - (TAPS // 2 - 1)).astype(jnp.int32)
        warped = warper(padded, row_start, col_start, tap_rows, tap_cols)
        return (summed + jnp.transpose(warped, (1, 0, 2, 3)), window_out)
    initial = jnp.zeros((BLOCKS, PLANES, BLOCK, BLOCK), jnp.float32)
    summed, correlation = lax.scan(one_volume, initial, (frames, shifts, fractions))
    return (correlation, summed * (1.0 / VOLS))

def partial_warp(block_size, taps):

    def warp_one(padded, row_start, col_start, tap_rows, tap_cols):
        return warp_block(padded, row_start, col_start, tap_rows, tap_cols, block_size, taps)
    return warp_one
```

```python
import numpy as np
import jax
import jax.numpy as jnp
from jax import lax
from jax.experimental import pallas as pl
from jax.experimental.pallas import tpu as pltpu
from jax.sharding import PartitionSpec as P

B = 128
NB = 32
BX = 8
F32 = jnp.float32
BF = jnp.bfloat16


def tables():
    n = np.arange(B)
    ang = 2 * np.pi * ((n[:, None] * n[None, :]) % B) / B
    cos, sin = np.cos(ang), -np.sin(ang)
    h = B // 2
    dr = np.zeros((2 * B, 2 * B))
    for v in range(2):
        dr[v * B : v * B + B, v * h : v * h + h] = cos[:, :h]
        dr[v * B : v * B + B, B + v * h : B + v * h + h] = sin[:, :h]
        dr[v * B : v * B + B, B + v * h] = cos[:, h]
    dc = np.block([[cos, -sin], [sin, cos]])
    lag = np.arange(32) - 16
    ay = 2 * np.pi * ((lag[:, None] * n[None, :]) % B) / B
    ey = np.block([[np.cos(ay), -np.sin(ay)], [np.sin(ay), np.cos(ay)]])
    ax = 2 * np.pi * ((n[:h, None] * lag[None, :]) % B) / B
    w = np.where(n[:h] == 0, 1.0, 2.0)[:, None] / B
    ex = np.zeros((2 * B, B))
    for v in range(2):
        ex[v * h : v * h + h, v * 32 : v * 32 + 32] = w * np.cos(ax)
        ex[B + v * h : B + v * h + h, v * 32 : v * 32 + 32] = -w * np.sin(ax)
        ex[B + v * h, v * 32 : v * 32 + 32] = np.where(lag % 2 == 0, 1.0, -1.0) / B
    i = np.arange(8) - 3
    t = i[None, :] - np.arange(16)[:, None] / 16
    raw = np.sinc(t) * np.sinc(t / 4)
    tap = raw / raw.sum(-1, keepdims=True)
    tap = np.concatenate([tap, np.zeros((16, 248))], 1)
    nn = np.arange(272)
    extc = tap[:, (nn[:, None] - n[None, :] - 5) % 256]
    nr, q = np.arange(144), np.arange(256)
    extr = tap[:, (q[None, :] - nr[:, None] - 5) % 256]
    extr = np.concatenate([extr[..., :B], extr[..., B:]], 0)
    return [np.asarray(x, np.float32).astype(BF) for x in (dr, dc, ey, ex, extc, extr)]


def dot(a, b):
    return jnp.dot(a, b, preferred_element_type=F32)


def lane(shape):
    return lax.broadcasted_iota(jnp.int32, shape, len(shape) - 1)


def row_stage(x0, x1, dr):
    return dot(jnp.concatenate([x0, x1], axis=1), dr)


def own_spectrum(y, dr, dc):
    r = row_stage(y, y, dr)
    rr, ri = r[:, :B], r[:, B:]
    ln = lane((B, B))
    rr2 = jnp.where(ln == 64, ri, rr)
    ri2 = jnp.where((ln == 64) | (ln == 0), 0.0, ri)
    f = dot(dc, jnp.concatenate([rr2, ri2], axis=0).astype(BF))
    fr, fi = f[:B], f[B:]
    main = jnp.where(ln < 64, fr, fi)
    main = jnp.where(ln == 64, pltpu.roll(fi, 64, 1), main)
    nr = jnp.transpose(fr)[64:72]
    ni = jnp.transpose(fi)[64:72]
    row = lax.broadcasted_iota(jnp.int32, (16, B), 0)
    nyq = jnp.where(row == 0, jnp.concatenate([nr, nr], axis=0),
                    pltpu.roll(jnp.concatenate([ni, ni], axis=0), 1, 0))
    return main.astype(BF), nyq.astype(BF)


def stage_tables(extc_b, extr_b, extc, extr):
    def body(f, _):
        extc[f] = extc_b[f].astype(F32)
        extr[f] = extr_b[f].astype(F32)
        extr[16 + f] = extr_b[16 + f].astype(F32)
        return 0
    lax.fori_loop(0, 16, body, 0)


def block_of(i):
    return (i % 8) * 4 + ((i // 8) % 2) * 2 + i // 16


def warp_block(i, codes, x, extc, extr):
    b = block_of(i)
    by, bx = b // BX, b % BX
    row0 = pl.multiple_of(by * B, B)
    col0 = pl.multiple_of(bx * B, B)
    ln = lane((160, B))
    zero = jnp.zeros((96, B), BF)
    total = None
    for v in range(2):
        cy, cx = codes[v, 0, b], codes[v, 1, b]
        sy, fy = jnp.right_shift(cy, 4), jnp.bitwise_and(cy, 15)
        sx, fx = jnp.right_shift(cx, 4), jnp.bitwise_and(cx, 15)
        acol = extc[fx, pl.ds(8 - sx, 256), :].astype(BF)
        arow = jnp.concatenate([extr[fy, pl.ds(8 + sy, 128), :].astype(BF), extr[16 + fy, pl.ds(8 + sy, 128), :].astype(BF)], axis=1)
        left = x[v, pl.ds(row0, 160), pl.ds(col0, B)]
        main = x[v, pl.ds(row0, 160), pl.ds(col0 + B, B)]
        right = x[v, pl.ds(row0, 160), pl.ds(col0 + 2 * B, B)]
        halo = jnp.where(ln < 64, right, left)
        t = dot(jnp.concatenate([main, halo], axis=1), acol).astype(BF)
        o = dot(arow, jnp.concatenate([t, zero], axis=0))
        total = o if total is None else total + o
    return total


def magnitude(re, im):
    sq = re * re + im * im
    return sq * lax.rsqrt(jnp.maximum(sq, 1e-37))


def front(i, x, dr, dc, r64):
    b = block_of(i)
    by, bx = b // BX, b % BX
    row0 = pl.multiple_of(by * B + 16, 16)
    col0 = pl.multiple_of(bx * B + B, B)
    ln = lane((B, B))
    r = row_stage(x[0, pl.ds(row0, B), pl.ds(col0, B)], x[1, pl.ds(row0, B), pl.ds(col0, B)], dr)
    rr, ri = r[:, :B], r[:, B:]
    half = jnp.bitwise_and(ln, 63)
    r64[...] = jnp.where(half == i, pltpu.roll(ri, i, 1), r64[...])
    ri = jnp.where(half == 0, 0.0, ri)
    return dot(dc, jnp.concatenate([rr.astype(BF), ri.astype(BF)], axis=0))


def cross(fr, fi, gr, gi):
    return fr * gr + fi * gi, fi * gr - fr * gi


def middle(b, f, gbuf, cr, ci, mg, sums):
    ln = lane((B, B))
    g = gbuf[b, 0:B, :].astype(F32)
    gs = pltpu.roll(g, 64, 1)
    gr = jnp.where(ln < 64, g, gs)
    gi = jnp.where(ln < 64, gs, g)
    re, im = cross(f[:B], f[B:], gr, gi)
    m = magnitude(re, im)
    cr[b], ci[b], mg[b] = re, im, m
    sums[pl.ds(b, 1), :] = jnp.sum(m, axis=0, keepdims=True)


def nyquist(gbuf, r64, dc, ey, sums, mean, q64):
    f = dot(dc, jnp.concatenate([r64[...].astype(BF), jnp.zeros((B, B), BF)], axis=0))
    z = jnp.zeros((32, B), F32)
    g = gbuf[:, B : B + 16, :].astype(F32)
    gr, gi = g[:, 0, :], g[:, 1, :]
    gr = jnp.transpose(jnp.concatenate([gr, z, gr, z], axis=0))
    gi = jnp.transpose(jnp.concatenate([gi, z, gi, z], axis=0))
    re, im = cross(f[:B], f[B:], gr, gi)
    m = magnitude(re, im)
    m64 = jnp.sum(m, axis=0, keepdims=True)
    ln = lane((NB, B))
    half = jnp.bitwise_and(ln, 63)
    diag = half == lax.broadcasted_iota(jnp.int32, (NB, B), 0)
    s = sums[...] * jnp.where(half == 0, 1.0, 2.0) + jnp.where(diag, m64, 0.0)
    s0 = jnp.sum(jnp.where(ln < 64, s, 0.0), axis=1, keepdims=True)
    s1 = jnp.sum(jnp.where(ln < 64, 0.0, s), axis=1, keepdims=True)
    mm = jnp.where(ln < 64, s0, s1) * (1.0 / (B * B)) + 1e-6
    mean[...] = mm
    mrow = jnp.sum(jnp.where(diag, mm, 0.0), axis=0, keepdims=True)
    live = jnp.bitwise_and(lane((1, B)), 63) < NB
    inv = 1.0 / (m + jnp.where(live, mrow, 1.0))
    w = jnp.concatenate([(re * inv).astype(BF), (im * inv).astype(BF)], axis=0)
    q64[...] = dot(ey, w)[0:32]


def back(i, codes, cr, ci, mg, mean, q64, ey, ex, win, flat):
    b = block_of(i)
    inv = 1.0 / (mg[i] + mean[pl.ds(i, 1), :])
    w = jnp.concatenate([(cr[i] * inv).astype(BF), (ci[i] * inv).astype(BF)], axis=0)
    q = dot(ey, w)
    half = jnp.bitwise_and(lane((32, B)), 63)
    qi = jnp.where(half == 0, pltpu.roll(q64[...], jnp.bitwise_and(B - i, B - 1), 1), q[32:64])
    c = dot(jnp.concatenate([q[0:32].astype(BF), qi.astype(BF)], axis=1), ex)
    win[i] = c
    for v in range(2):
        sy = jnp.right_shift(codes[v, 0, b], 4)
        sx = jnp.right_shift(codes[v, 1, b], 4)
        piece = win[i, pl.ds(sy + 8, 16), :]
        piece = pltpu.roll(piece, jnp.bitwise_and(B - (8 + 32 * v) - sx, B - 1), 1)
        row = (b // 4) * 8 + v * 4 + b % 4
        flat[pl.ds(row, 16, stride=64), :] = piece


def flatten(flat):
    ln = lane((64, B))
    tiles = []
    for t in range(2):
        out = None
        for k in range(8):
            a = t * 8 + k
            piece = flat[a * 64 : a * 64 + 64, :]
            if k:
                piece = pltpu.roll(piece, 16 * k, 1)
            out = piece if out is None else jnp.where(ln >= 16 * k, piece, out)
        tiles.append(out)
    return tiles


MESH = pl.DeviceIdType.MESH
VM = pl.BlockSpec(memory_space=pltpu.VMEM)
ANY = pl.BlockSpec(memory_space=pl.ANY)
SM = pl.BlockSpec(memory_space=pltpu.SMEM)
UN = 4


def place():
    tm = lax.axis_index("tm")
    return tm // 4, (tm // 2) % 2, tm % 2, lax.axis_index("plane")


def at(z, yh, c, p):
    return (z * 4 + yh * 2 + c, p)


def partners(with_plane):
    z, yh, c, p = place()
    ids = [at((z + d) % 8, yh, c, p) for d in range(1, 8)]
    ids += [at(z, 1 - yh, c, p), at(z, yh, 1 - c, p)]
    if with_plane:
        ids += [at(z, yh, c, (p + d) % 8) for d in range(1, 8)]
    return ids


def greet(with_plane):
    sem = pltpu.get_barrier_semaphore()
    ids = partners(with_plane)
    for dev in ids:
        pl.semaphore_signal(sem, inc=1, device_id=dev, device_id_type=MESH)
    pl.semaphore_wait(sem, len(ids))


def remote(src, dst, send, recv, dev):
    return pltpu.make_async_remote_copy(
        src_ref=src, dst_ref=dst, send_sem=send, recv_sem=recv, device_id=dev, device_id_type=MESH
    )


def gather_kernel(y, dr, dc, out, g, send, recv):
    z, yh, c, p = place()
    mine = c * 16 + yh * 8 + z
    main, nyq = own_spectrum(y[0, 0], dr[...], dc[...])
    g[mine, 0:B, :] = main
    g[mine, B : B + 16, :] = nyq
    greet(False)
    first = []
    for d in range(1, 8):
        cp = remote(g.at[mine], g.at[mine], send.at[d], recv.at[d], at((z + d) % 8, yh, c, p))
        cp.start()
        first.append(cp)
    for cp in first:
        cp.wait()
    own = pl.ds(c * 16 + yh * 8, 8)
    cp = remote(g.at[own], g.at[own], send.at[8], recv.at[8], at(z, 1 - yh, c, p))
    cp.start()
    cp.wait()
    own = pl.ds(c * 16, 16)
    cp = remote(g.at[own], g.at[own], send.at[9], recv.at[9], at(z, yh, 1 - c, p))
    cp.start()
    cp.wait()
    out[...] = g[...]


def zero_pads(x):
    x[:, 0:16, :] = jnp.zeros((2, 16, 1280), BF)
    x[:, 528:544, :] = jnp.zeros((2, 16, 1280), BF)
    x[:, :, 0:B] = jnp.zeros((2, 544, B), BF)
    x[:, :, 1152:1280] = jnp.zeros((2, 544, B), BF)


def compute_kernel(codes, frames, g, dr, dc, ey, ex, extc_b, extr_b, part, corr,
                   x, extc, extr, r64, cr, ci, mg, sums, mean, q64, win, flat, sem):
    cp = pltpu.make_async_copy(frames.at[:, 0], x.at[:, 16:528, B:1152], sem)
    cp.start()
    zero_pads(x)
    stage_tables(extc_b, extr_b, extc, extr)
    r64[...] = jnp.zeros_like(r64)
    cp.wait()

    def warp_step(i, _):
        part[i] = warp_block(i, codes, x, extc, extr).astype(BF)
        return 0

    def front_step(i, _):
        f = front(i, x, dr[...], dc[...], r64)
        middle(i, f, g, cr, ci, mg, sums)
        return 0

    def back_step(i, _):
        back(i, codes, cr, ci, mg, mean, q64, ey[...], ex[...], win, flat)
        return 0

    lax.fori_loop(0, NB, warp_step, 0, unroll=UN)
    lax.fori_loop(0, NB, front_step, 0, unroll=UN)
    nyquist(g, r64, dc[...], ey[...], sums, mean, q64)
    lax.fori_loop(0, NB, back_step, 0, unroll=UN)
    t = flatten(flat)
    corr[:, 0:B] = t[0]
    corr[:, B : 2 * B] = t[1]


def reduce_kernel(part, corr, out_c, out_t, ra, sb, rb, sc, rc, rp, send, recv):
    z, yh, c, p = place()
    greet(True)
    far = []
    for d in range(1, 8):
        q = (p + d) % 8
        cp = remote(corr.at[pl.ds(pl.multiple_of(q * 8, 8), 8)], rp.at[d - 1], send.at[d], recv.at[d], at(z, yh, c, q))
        cp.start()
        far.append(cp)
    cp = remote(part.at[pl.ds((1 - c) * 16, 16)], ra, send.at[8], recv.at[8], at(z, yh, 1 - c, p))
    cp.start()
    cp.wait()

    def add_a(j, _):
        sb[j] = (part[c * 16 + j].astype(F32) + ra[j].astype(F32)).astype(BF)
        return 0

    lax.fori_loop(0, 16, add_a, 0)
    cp = remote(sb.at[pl.ds((1 - yh) * 8, 8)], rb, send.at[9], recv.at[9], at(z, 1 - yh, c, p))
    cp.start()
    cp.wait()

    def add_b(j, _):
        sc[j] = (sb[yh * 8 + j].astype(F32) + rb[j].astype(F32)).astype(BF)
        return 0

    lax.fori_loop(0, 8, add_b, 0)
    near = []
    for d in range(1, 8):
        q = (z + d) % 8
        cp = remote(sc.at[q], rc.at[d - 1], send.at[9 + d], recv.at[9 + d], at(q, yh, c, p))
        cp.start()
        near.append(cp)
    for cp in far:
        cp.wait()
    total = corr[pl.ds(pl.multiple_of(p * 8, 8), 8), :]
    for d in range(7):
        total = total + rp[d]
    out_c[...] = total
    for cp in near:
        cp.wait()
    total = sc[z].astype(F32)
    for d in range(7):
        total = total + rc[d].astype(F32)
    out_t[...] = total * (1.0 / 64)


def on_device(frames, template, codes):
    dr, dc, ey, ex, extc, extr = tables()
    big = pltpu.CompilerParams(vmem_limit_bytes=60 * 2**20)
    dma = pltpu.SemaphoreType.DMA
    g = pl.pallas_call(
        gather_kernel,
        out_shape=jax.ShapeDtypeStruct((NB, 144, B), BF),
        in_specs=[VM] * 3, out_specs=VM,
        scratch_shapes=[pltpu.VMEM((NB, 144, B), BF), dma((10,)), dma((10,))],
        compiler_params=pltpu.CompilerParams(collective_id=0, has_side_effects=True),
    )(template, dr, dc)
    part, corr = pl.pallas_call(
        compute_kernel,
        out_shape=[jax.ShapeDtypeStruct((NB, B, B), BF), jax.ShapeDtypeStruct((64, 256), F32)],
        in_specs=[SM, ANY] + [VM] * 7, out_specs=[VM, VM],
        scratch_shapes=[
            pltpu.VMEM((2, 544, 1280), BF), pltpu.VMEM((16, 272, B), F32), pltpu.VMEM((32, 144, B), F32),
            pltpu.VMEM((B, B), F32), pltpu.VMEM((NB, B, B), F32), pltpu.VMEM((NB, B, B), F32), pltpu.VMEM((NB, B, B), F32),
            pltpu.VMEM((NB, B), F32), pltpu.VMEM((NB, B), F32), pltpu.VMEM((32, B), F32),
            pltpu.VMEM((NB, 32, B), F32), pltpu.VMEM((1024, B), F32), dma,
        ],
        compiler_params=big,
    )(codes, frames, g, dr, dc, ey, ex, extc, extr)
    out_c, out_t = pl.pallas_call(
        reduce_kernel,
        out_shape=[jax.ShapeDtypeStruct((8, 256), F32), jax.ShapeDtypeStruct((B, B), F32)],
        in_specs=[VM, VM], out_specs=[VM, VM],
        scratch_shapes=[
            pltpu.VMEM((16, B, B), BF), pltpu.VMEM((16, B, B), BF), pltpu.VMEM((8, B, B), BF), pltpu.VMEM((8, B, B), BF),
            pltpu.VMEM((7, B, B), BF), pltpu.VMEM((7, 8, 256), F32), dma((17,)), dma((17,)),
        ],
        compiler_params=pltpu.CompilerParams(collective_id=1, has_side_effects=True, vmem_limit_bytes=32 * 2**20),
    )(part, corr)
    return out_c.reshape(2, 4, 256), out_t.reshape(1, 1, B, B)


def solution(mesh):
    in_specs = (P("tm", "plane", None, None), P("tm", "plane", None, None), P("tm", None, None))
    out_specs = (P("tm", "plane", None), P("tm", "plane", None, None))
    return jax.shard_map(on_device, mesh=mesh, in_specs=in_specs, out_specs=out_specs, check_vma=False)
```

```python
import numpy as np
import jax
import jax.numpy as jnp
from jax import lax
from jax.experimental import pallas as pl
from jax.experimental.pallas import tpu as pltpu
from jax.sharding import PartitionSpec as P

B = 128
NB = 32
BX = 8
F32 = jnp.float32
BF = jnp.bfloat16


def tables():
    n = np.arange(B)
    ang = 2 * np.pi * ((n[:, None] * n[None, :]) % B) / B
    cos, sin = np.cos(ang), -np.sin(ang)
    h = B // 2
    dr = np.zeros((2 * B, 2 * B))
    for v in range(2):
        dr[v * B : v * B + B, v * h : v * h + h] = cos[:, :h]
        dr[v * B : v * B + B, B + v * h : B + v * h + h] = sin[:, :h]
        dr[v * B : v * B + B, B + v * h] = cos[:, h]
    dc = np.block([[cos, -sin], [sin, cos]])
    lag = np.arange(32) - 16
    ay = 2 * np.pi * ((lag[:, None] * n[None, :]) % B) / B
    ey = np.block([[np.cos(ay), -np.sin(ay)], [np.sin(ay), np.cos(ay)]])
    ax = 2 * np.pi * ((n[:h, None] * lag[None, :]) % B) / B
    w = np.where(n[:h] == 0, 1.0, 2.0)[:, None] / B
    ex = np.zeros((2 * B, B))
    for v in range(2):
        ex[v * h : v * h + h, v * 32 : v * 32 + 32] = w * np.cos(ax)
        ex[B + v * h : B + v * h + h, v * 32 : v * 32 + 32] = -w * np.sin(ax)
        ex[B + v * h, v * 32 : v * 32 + 32] = np.where(lag % 2 == 0, 1.0, -1.0) / B
    i = np.arange(8) - 3
    t = i[None, :] - np.arange(16)[:, None] / 16
    raw = np.sinc(t) * np.sinc(t / 4)
    tap = raw / raw.sum(-1, keepdims=True)
    tap = np.concatenate([tap, np.zeros((16, 248))], 1)
    nn = np.arange(272)
    extc = tap[:, (nn[:, None] - n[None, :] - 5) % 256]
    nr, q = np.arange(144), np.arange(256)
    extr = tap[:, (q[None, :] - nr[:, None] - 5) % 256]
    ext = np.concatenate([extc[:, :144], extc[:, 256:272], extr[..., :B], extr[:, 112:144, B:]], 1)
    return [np.asarray(x, np.float32).astype(BF) for x in (dr, dc, ey, ex, ext)]


def dot(a, b):
    return jnp.dot(a, b, preferred_element_type=F32)


def lane(shape):
    return lax.broadcasted_iota(jnp.int32, shape, len(shape) - 1)


def row_stage(x0, x1, dr):
    return dot(jnp.concatenate([x0, x1], axis=1), dr)


def own_spectrum(y, dr, dc):
    r = row_stage(y, y, dr)
    rr, ri = r[:, :B], r[:, B:]
    ln = lane((B, B))
    rr2 = jnp.where(ln == 64, ri, rr)
    ri2 = jnp.where((ln == 64) | (ln == 0), 0.0, ri)
    f = dot(dc, jnp.concatenate([rr2, ri2], axis=0).astype(BF))
    fr, fi = f[:B], f[B:]
    main = jnp.where(ln < 64, fr, fi)
    main = jnp.where(ln == 64, pltpu.roll(fi, 64, 1), main)
    nr = jnp.transpose(fr)[64:72]
    ni = jnp.transpose(fi)[64:72]
    row = lax.broadcasted_iota(jnp.int32, (16, B), 0)
    nyq = jnp.where(row == 0, jnp.concatenate([nr, nr], axis=0),
                    pltpu.roll(jnp.concatenate([ni, ni], axis=0), 1, 0))
    return main.astype(BF), nyq.astype(BF)


def stage_tables(ext, extc, extr):
    zero = jnp.zeros((112, B), F32)

    def body(f, _):
        extc[f, 0:144] = ext[f, 0:144].astype(F32)
        extc[f, 144:256] = zero
        extc[f, 256:272] = ext[f, 144:160].astype(F32)
        extr[f] = ext[f, 160:304].astype(F32)
        extr[16 + f, 0:112] = zero
        extr[16 + f, 112:144] = ext[f, 304:336].astype(F32)
        return 0

    lax.fori_loop(0, 16, body, 0)


def block_of(i):
    return (i % 8) * 4 + ((i // 8) % 2) * 2 + i // 16


def warp_block(i, codes, x, extc, extr):
    b = block_of(i)
    by, bx = b // BX, b % BX
    row0 = pl.multiple_of(by * B, B)
    col0 = pl.multiple_of(bx * B, B)
    ln = lane((160, B))
    zero = jnp.zeros((96, B), BF)
    total = None
    for v in range(2):
        cy, cx = codes[v, 0, b], codes[v, 1, b]
        sy, fy = jnp.right_shift(cy, 4), jnp.bitwise_and(cy, 15)
        sx, fx = jnp.right_shift(cx, 4), jnp.bitwise_and(cx, 15)
        acol = extc[fx, pl.ds(8 - sx, 256), :].astype(BF)
        arow = jnp.concatenate([extr[fy, pl.ds(8 + sy, 128), :].astype(BF), extr[16 + fy, pl.ds(8 + sy, 128), :].astype(BF)], axis=1)
        left = x[v, pl.ds(row0, 160), pl.ds(col0, B)]
        main = x[v, pl.ds(row0, 160), pl.ds(col0 + B, B)]
        right = x[v, pl.ds(row0, 160), pl.ds(col0 + 2 * B, B)]
        halo = jnp.where(ln < 64, right, left)
        t = dot(jnp.concatenate([main, halo], axis=1), acol).astype(BF)
        o = dot(arow, jnp.concatenate([t, zero], axis=0))
        total = o if total is None else total + o
    return total


def magnitude(re, im):
    sq = re * re + im * im
    return sq * lax.rsqrt(jnp.maximum(sq, 1e-37))


def front(i, x, dr, dc, r64, cr, ci):
    b = block_of(i)
    by, bx = b // BX, b % BX
    row0 = pl.multiple_of(by * B + 16, 16)
    col0 = pl.multiple_of(bx * B + B, B)
    ln = lane((B, B))
    r = row_stage(x[0, pl.ds(row0, B), pl.ds(col0, B)], x[1, pl.ds(row0, B), pl.ds(col0, B)], dr)
    rr, ri = r[:, :B], r[:, B:]
    half = jnp.bitwise_and(ln, 63)
    r64[...] = jnp.where(half == i, pltpu.roll(ri, i, 1), r64[...])
    ri = jnp.where(half == 0, 0.0, ri)
    f = dot(dc, jnp.concatenate([rr.astype(BF), ri.astype(BF)], axis=0))
    cr[i] = f[:B]
    ci[i] = f[B:]


def cross(fr, fi, gr, gi):
    return fr * gr + fi * gi, fi * gr - fr * gi


def middle(b, gbuf, cr, ci, mg, sums):
    ln = lane((B, B))
    g = gbuf[b, 0:B, :].astype(F32)
    gs = pltpu.roll(g, 64, 1)
    gr = jnp.where(ln < 64, g, gs)
    gi = jnp.where(ln < 64, gs, g)
    re, im = cross(cr[b], ci[b], gr, gi)
    m = magnitude(re, im)
    cr[b], ci[b], mg[b] = re, im, m
    sums[pl.ds(b, 1), :] = jnp.sum(m, axis=0, keepdims=True)


def nyquist(gbuf, r64, dc, ey, sums, mean, q64):
    f = dot(dc, jnp.concatenate([r64[...].astype(BF), jnp.zeros((B, B), BF)], axis=0))
    z = jnp.zeros((32, B), F32)
    g = gbuf[:, B : B + 16, :].astype(F32)
    gr, gi = g[:, 0, :], g[:, 1, :]
    gr = jnp.transpose(jnp.concatenate([gr, z, gr, z], axis=0))
    gi = jnp.transpose(jnp.concatenate([gi, z, gi, z], axis=0))
    re, im = cross(f[:B], f[B:], gr, gi)
    m = magnitude(re, im)
    m64 = jnp.sum(m, axis=0, keepdims=True)
    ln = lane((NB, B))
    half = jnp.bitwise_and(ln, 63)
    diag = half == lax.broadcasted_iota(jnp.int32, (NB, B), 0)
    s = sums[...] * jnp.where(half == 0, 1.0, 2.0) + jnp.where(diag, m64, 0.0)
    s0 = jnp.sum(jnp.where(ln < 64, s, 0.0), axis=1, keepdims=True)
    s1 = jnp.sum(jnp.where(ln < 64, 0.0, s), axis=1, keepdims=True)
    mm = jnp.where(ln < 64, s0, s1) * (1.0 / (B * B)) + 1e-6
    mean[...] = mm
    mrow = jnp.sum(jnp.where(diag, mm, 0.0), axis=0, keepdims=True)
    live = jnp.bitwise_and(lane((1, B)), 63) < NB
    inv = 1.0 / (m + jnp.where(live, mrow, 1.0))
    w = jnp.concatenate([(re * inv).astype(BF), (im * inv).astype(BF)], axis=0)
    q64[...] = dot(ey, w)[0:32]


def back(k, zt, codes, cr, ci, mg, mean, q64, ey, ex, win, flat):
    i = k * 8 + zt
    b = block_of(i)
    inv = 1.0 / (mg[i] + mean[pl.ds(i, 1), :])
    w = jnp.concatenate([(cr[i] * inv).astype(BF), (ci[i] * inv).astype(BF)], axis=0)
    q = dot(ey, w)
    half = jnp.bitwise_and(lane((32, B)), 63)
    qi = jnp.where(half == 0, pltpu.roll(q64[...], jnp.bitwise_and(B - i, B - 1), 1), q[32:64])
    win[k] = dot(jnp.concatenate([q[0:32].astype(BF), qi.astype(BF)], axis=1), ex)
    for v in range(2):
        sy = jnp.right_shift(codes[v, 0, b], 4)
        sx = jnp.right_shift(codes[v, 1, b], 4)
        piece = win[k, pl.ds(sy + 8, 16), :]
        piece = pltpu.roll(piece, jnp.bitwise_and(B - (8 + 32 * v) - sx, B - 1), 1)
        row = v * 4 + (k % 2) * 2 + k // 2
        flat[pl.ds(row, 16, stride=8), :] = piece


def flatten(flat):
    ln = lane((8, B))
    tiles = []
    for t in range(2):
        out = None
        for k in range(8):
            a = t * 8 + k
            piece = flat[a * 8 : a * 8 + 8, :]
            if k:
                piece = pltpu.roll(piece, 16 * k, 1)
            out = piece if out is None else jnp.where(ln >= 16 * k, piece, out)
        tiles.append(out)
    return jnp.concatenate(tiles, axis=1)


MESH = pl.DeviceIdType.MESH
ANY = pl.BlockSpec(memory_space=pl.ANY)
VM = pl.BlockSpec(memory_space=pltpu.VMEM)
SM = pl.BlockSpec(memory_space=pltpu.SMEM)
NEAR = (1, 7, 2, 6, 3, 5, 4)
FAR = (4, 3, 5, 2, 6, 1, 7, 0)
GZ, GY, GS, SA, SY, SZ, CP, NSEM = 0, 8, 16, 32, 34, 42, 50, 58


def kernel(codes, frames, y_h, dr_h, dc_h, ey_h, ex_h, ext_h, out_c, out_t,
           x, ext, extc, extr, y, dr, dc, ey, ex, g, r64, cr, ci, mg, sums, mean, q64, win, flat, sent,
           part, ra, sb, rb, sc, rc, rp, own, local, send, recv):
    tm = lax.axis_index("tm")
    z, yh, c, p = tm // 4, (tm // 2) % 2, tm % 2, lax.axis_index("plane")

    def at(zz, yy, cc, pp):
        return (zz * 4 + yy * 2 + cc, pp)

    up = [at((z + d) % 8, yh, c, p) for d in range(8)]
    across, sibling = at(z, 1 - yh, c, p), at(z, yh, 1 - c, p)
    peers = [at(z, yh, c, (p + d) % 8) for d in range(8)]

    def slot(cc, yy, zz):
        return cc * 16 + yy * 8 + zz

    def copy(src, dst, sem, dev):
        return pltpu.make_async_remote_copy(
            src_ref=src, dst_ref=dst, send_sem=send.at[sem], recv_sem=recv.at[sem],
            device_id=dev, device_id_type=MESH)

    def spectrum_copy(at_slot, sem, dev):
        return copy(g.at[at_slot], g.at[at_slot], sem, dev)

    barrier = pltpu.get_barrier_semaphore()
    greeted = up[1:] + [across, sibling] + peers[1:]
    for dev in greeted:
        pl.semaphore_signal(barrier, inc=1, device_id=dev, device_id_type=MESH)
    loads = [pltpu.make_async_copy(a, b, local.at[n]) for n, (a, b) in enumerate(
        ((y_h.at[0, 0], y), (dr_h, dr), (dc_h, dc), (ext_h, ext),
         (frames.at[:, 0], x.at[:, 16:528, B:1152]), (ey_h, ey), (ex_h, ex)))]
    for cp in loads:
        cp.start()
    x[:, 0:16, :] = jnp.zeros((2, 16, 1280), BF)
    x[:, 528:544, :] = jnp.zeros((2, 16, 1280), BF)
    x[:, 16:528, 0:B] = jnp.zeros((2, 512, B), BF)
    x[:, 16:528, 1152:1280] = jnp.zeros((2, 512, B), BF)
    r64[...] = jnp.zeros_like(r64)
    for cp in loads[:3]:
        cp.wait()
    mine = slot(c, yh, z)
    main, nyq = own_spectrum(y[...], dr[...], dc[...])
    g[mine, 0:B, :] = main
    g[mine, B : B + 16, :] = nyq
    loads[3].wait()
    stage_tables(ext, extc, extr)
    pl.semaphore_wait(barrier, len(greeted))
    for d in NEAR:
        spectrum_copy(mine, GZ + d, up[d]).start()
    spectrum_copy(mine, GY, across).start()
    spectrum_copy(mine, GS, sibling).start()
    for cp in loads[4:]:
        cp.wait()

    def z_arrived(d):
        s = slot(c, yh, (z + 8 - d) % 8)
        spectrum_copy(s, GZ + d, up[d]).wait_recv()
        spectrum_copy(s, GY + d, across).start()
        spectrum_copy(s, GS + d, sibling).start()

    def y_arrived(d):
        s = slot(c, 1 - yh, (z + 8 - d) % 8)
        spectrum_copy(s, GY + d, across).wait_recv()
        spectrum_copy(s, GS + 8 + d, sibling).start()

    def sibling_arrived(k):
        for d in range(8):
            s = slot(1 - c, yh if k == 0 else 1 - yh, (z + 8 - d) % 8)
            spectrum_copy(s, GS + 8 * k + d, sibling).wait_recv()

    def sum_a(n):
        return copy(part.at[pl.ds(8 * n, 8)], ra.at[pl.ds(8 * n, 8)], SA + n, sibling)

    def sum_y(d):
        t = (z + d) % 8
        return copy(sb.at[t], rb.at[t], SY + d, across)

    def sum_z(d):
        return copy(sc.at[(z + d) % 8], rc.at[d - 1], SZ + d, up[d])

    def both(w):
        return part[16 + w].astype(F32) + ra[w].astype(F32)

    def send_y():
        sum_a(0).wait_recv()
        for d in FAR:
            t = (z + d) % 8
            sb[t] = both(t).astype(BF)
        for d in FAR:
            sum_y(d).start()

    def send_z(ds):
        for d in ds:
            sum_y(d).wait_recv()
            t = (z + d) % 8
            total = both(8 + t) + rb[t].astype(F32)
            if d == 0:
                own[...] = total
            else:
                sc[t] = total.astype(BF)
                sum_z(d).start()

    def slot_of(w):
        cc = jnp.where(w < 16, 1 - c, c)
        yy = jnp.where((w // 8) % 2 == 0, 1 - yh, yh)
        return cc * 16 + yy * 8 + w % 8

    def phase(step, events, order):
        def quarter(n, _):
            q = n if order else 3 - n

            def one(j, _):
                step(q * 8 + j)
                return 0

            lax.fori_loop(0, 8, one, 0, unroll=UN)
            for k, event in events.items():
                pl.when(n == k)(event)
            return 0

        lax.fori_loop(0, 4, quarter, 0)

    def warp_step(w):
        part[w] = warp_block(slot_of(w), codes, x, extc, extr).astype(BF)

    def after_1():
        sum_a(1).start()
        z_arrived(1)
        z_arrived(7)

    def after_2():
        send_y()
        z_arrived(2)
        z_arrived(6)

    def after_3():
        z_arrived(3)
        z_arrived(5)

    phase(warp_step, {0: lambda: sum_a(0).start(), 1: after_1, 2: after_2, 3: after_3}, True)

    def front_step(w):
        front(slot_of(w), x, dr[...], dc[...], r64, cr, ci)

    def front_0():
        z_arrived(4)
        y_arrived(0)

    def arrivals(*ds):
        def event():
            for d in ds:
                y_arrived(d)
        return event

    phase(front_step, {0: front_0, 1: arrivals(1, 7), 2: arrivals(2, 6), 3: arrivals(3, 5, 4)}, True)

    def middle_step(w):
        middle(slot_of(w), g, cr, ci, mg, sums)

    def middle_0():
        sum_a(1).wait_recv()
        send_z(FAR[:4])

    def middle_1():
        send_z(FAR[4:])
        sibling_arrived(0)

    phase(middle_step, {0: middle_0, 1: middle_1, 2: lambda: sibling_arrived(1)}, False)
    nyquist(g, r64, dc[...], ey[...], sums, mean, q64)

    def window_copy(d):
        return copy(sent.at[d], rp.at[d - 1], CP + d, peers[d])

    def back_step(n, _):
        zt = (p + 1 + n) % 8
        for k in range(4):
            back(k, zt, codes, cr, ci, mg, mean, q64, ey[...], ex[...], win, flat)
        sent[(n + 1) % 8] = flatten(flat)
        for d in range(1, 8):
            pl.when(n == d - 1)(lambda d=d: window_copy(d).start())
        return 0

    lax.fori_loop(0, 8, back_step, 0)
    for d in range(1, 8):
        sum_z(d).wait_recv()
    total = own[...]
    for d in range(7):
        total = total + rc[d].astype(F32)
    out_t[0, 0] = total * (1.0 / 64)
    for d in range(1, 8):
        window_copy(d).wait_recv()
    total = sent[0]
    for d in range(7):
        total = total + rp[d]
    out_c[0] = total[0:4]
    out_c[1] = total[4:8]
    for d in range(1, 8):
        spectrum_copy(mine, GZ + d, up[d]).wait_send()
        sum_z(d).wait_send()
        window_copy(d).wait_send()
    for d in range(8):
        spectrum_copy(mine, GY + d, across).wait_send()
        spectrum_copy(mine, GS + d, sibling).wait_send()
        spectrum_copy(mine, GS + 8 + d, sibling).wait_send()
        sum_y(d).wait_send()
    sum_a(0).wait_send()
    sum_a(1).wait_send()


UN = 4


def on_device(frames, template, codes):
    vm = pltpu.VMEM
    dma = pltpu.SemaphoreType.DMA
    return pl.pallas_call(
        kernel,
        out_shape=[jax.ShapeDtypeStruct((2, 4, 256), F32), jax.ShapeDtypeStruct((1, 1, B, B), F32)],
        in_specs=[SM] + [ANY] * 7,
        out_specs=[VM, VM],
        scratch_shapes=[
            vm((2, 544, 1280), BF), vm((16, 336, B), BF), vm((16, 272, B), F32), vm((32, 144, B), F32),
            vm((B, B), BF), vm((2 * B, 2 * B), BF), vm((2 * B, 2 * B), BF), vm((64, 2 * B), BF), vm((2 * B, B), BF),
            vm((NB, 144, B), BF), vm((B, B), F32),
            vm((NB, B, B), F32), vm((NB, B, B), F32), vm((NB, B, B), F32),
            vm((NB, B), F32), vm((NB, B), F32), vm((32, B), F32),
            vm((4, 32, B), F32), vm((B, B), F32), vm((8, 8, 2 * B), F32),
            vm((NB, B, B), BF), vm((16, B, B), BF), vm((8, B, B), BF), vm((8, B, B), BF),
            vm((8, B, B), BF), vm((7, B, B), BF), vm((7, 8, 2 * B), F32), vm((B, B), F32),
            dma((7,)), dma((NSEM,)), dma((NSEM,)),
        ],
        compiler_params=pltpu.CompilerParams(
            collective_id=0, has_side_effects=True, vmem_limit_bytes=48 * 2**20),
    )(codes, frames, template, *tables())


def solution(mesh):
    in_specs = (P("tm", "plane", None, None), P("tm", "plane", None, None), P("tm", None, None))
    out_specs = (P("tm", "plane", None), P("tm", "plane", None, None))
    return jax.shard_map(on_device, mesh=mesh, in_specs=in_specs, out_specs=out_specs, check_vma=False)
```

```python
import numpy as np
import jax
import jax.numpy as jnp
from jax import lax
from jax.experimental import pallas as pl
from jax.experimental.pallas import tpu as pltpu
from jax.sharding import PartitionSpec as P

B = 128
NB = 32
BX = 8
F32 = jnp.float32
BF = jnp.bfloat16


def tables():
    n = np.arange(B)
    ang = 2 * np.pi * ((n[:, None] * n[None, :]) % B) / B
    cos, sin = np.cos(ang), -np.sin(ang)
    h = B // 2
    dr = np.zeros((2 * B, 2 * B))
    for v in range(2):
        dr[v * B : v * B + B, v * h : v * h + h] = cos[:, :h]
        dr[v * B : v * B + B, B + v * h : B + v * h + h] = sin[:, :h]
        dr[v * B : v * B + B, B + v * h] = cos[:, h]
    dc = np.block([[cos, -sin], [sin, cos]])
    lag = np.arange(32) - 16
    ay = 2 * np.pi * ((lag[:, None] * n[None, :]) % B) / B
    ey = np.block([[np.cos(ay), -np.sin(ay)], [np.sin(ay), np.cos(ay)]])
    ax = 2 * np.pi * ((n[:h, None] * lag[None, :]) % B) / B
    w = np.where(n[:h] == 0, 1.0, 2.0)[:, None] / B
    ex = np.zeros((2 * B, B))
    for v in range(2):
        ex[v * h : v * h + h, v * 32 : v * 32 + 32] = w * np.cos(ax)
        ex[B + v * h : B + v * h + h, v * 32 : v * 32 + 32] = -w * np.sin(ax)
        ex[B + v * h, v * 32 : v * 32 + 32] = np.where(lag % 2 == 0, 1.0, -1.0) / B
    i = np.arange(8) - 3
    t = i[None, :] - np.arange(16)[:, None] / 16
    raw = np.sinc(t) * np.sinc(t / 4)
    tap = raw / raw.sum(-1, keepdims=True)
    tap = np.concatenate([tap, np.zeros((16, 248))], 1)
    nn = np.arange(272)
    extc = tap[:, (nn[:, None] - n[None, :] - 5) % 256]
    nr, q = np.arange(144), np.arange(256)
    extr = tap[:, (q[None, :] - nr[:, None] - 5) % 256]
    ext = np.concatenate([extc[:, :144], extc[:, 256:272], extr[..., :B], extr[:, 112:144, B:]], 1)
    return [np.asarray(x, np.float32).astype(BF) for x in (dr, dc, ey, ex, ext)]


def dot(a, b):
    return jnp.dot(a, b, preferred_element_type=F32)


def lane(shape):
    return lax.broadcasted_iota(jnp.int32, shape, len(shape) - 1)


def row_stage(x0, x1, dr):
    return dot(jnp.concatenate([x0, x1], axis=1), dr)


def own_spectrum(y, dr, dc):
    r = row_stage(y, y, dr)
    rr, ri = r[:, :B], r[:, B:]
    ln = lane((B, B))
    rr2 = jnp.where(ln == 64, ri, rr)
    ri2 = jnp.where((ln == 64) | (ln == 0), 0.0, ri)
    f = dot(dc, jnp.concatenate([rr2, ri2], axis=0).astype(BF))
    fr, fi = f[:B], f[B:]
    main = jnp.where(ln < 64, fr, fi)
    main = jnp.where(ln == 64, pltpu.roll(fi, 64, 1), main)
    nr = jnp.transpose(fr)[64:72]
    ni = jnp.transpose(fi)[64:72]
    row = lax.broadcasted_iota(jnp.int32, (16, B), 0)
    nyq = jnp.where(row == 0, jnp.concatenate([nr, nr], axis=0),
                    pltpu.roll(jnp.concatenate([ni, ni], axis=0), 1, 0))
    return main.astype(BF), nyq.astype(BF)


def stage_tables(ext, extc, extr):
    zero = jnp.zeros((112, B), F32)

    def body(f, _):
        extc[f, 0:144] = ext[f, 0:144].astype(F32)
        extc[f, 144:256] = zero
        extc[f, 256:272] = ext[f, 144:160].astype(F32)
        extr[f] = ext[f, 160:304].astype(F32)
        extr[16 + f, 0:112] = zero
        extr[16 + f, 112:144] = ext[f, 304:336].astype(F32)
        return 0

    lax.fori_loop(0, 16, body, 0)


def block_of(i):
    return (i % 8) * 4 + ((i // 8) % 2) * 2 + i // 16


def warp_block(i, codes, x, extc, extr):
    b = block_of(i)
    by, bx = b // BX, b % BX
    row0 = pl.multiple_of(by * B, B)
    col0 = pl.multiple_of(bx * B, B)
    ln = lane((160, B))
    zero = jnp.zeros((96, B), BF)
    total = None
    for v in range(2):
        cy, cx = codes[v, 0, b], codes[v, 1, b]
        sy, fy = jnp.right_shift(cy, 4), jnp.bitwise_and(cy, 15)
        sx, fx = jnp.right_shift(cx, 4), jnp.bitwise_and(cx, 15)
        acol = extc[fx, pl.ds(8 - sx, 256), :].astype(BF)
        arow = jnp.concatenate([extr[fy, pl.ds(8 + sy, 128), :].astype(BF), extr[16 + fy, pl.ds(8 + sy, 128), :].astype(BF)], axis=1)
        left = x[v, pl.ds(row0, 160), pl.ds(col0, B)]
        main = x[v, pl.ds(row0, 160), pl.ds(col0 + B, B)]
        right = x[v, pl.ds(row0, 160), pl.ds(col0 + 2 * B, B)]
        halo = jnp.where(ln < 64, right, left)
        t = dot(jnp.concatenate([main, halo], axis=1), acol).astype(BF)
        o = dot(arow, jnp.concatenate([t, zero], axis=0))
        total = o if total is None else total + o
    return total


def magnitude(re, im):
    sq = re * re + im * im
    return sq * lax.rsqrt(jnp.maximum(sq, 1e-37))


def front(i, x, dr, dc, r64, cr, ci):
    b = block_of(i)
    by, bx = b // BX, b % BX
    row0 = pl.multiple_of(by * B + 16, 16)
    col0 = pl.multiple_of(bx * B + B, B)
    ln = lane((B, B))
    r = row_stage(x[0, pl.ds(row0, B), pl.ds(col0, B)], x[1, pl.ds(row0, B), pl.ds(col0, B)], dr)
    rr, ri = r[:, :B], r[:, B:]
    half = jnp.bitwise_and(ln, 63)
    r64[...] = jnp.where(half == i, pltpu.roll(ri, i, 1), r64[...])
    ri = jnp.where(half == 0, 0.0, ri)
    f = dot(dc, jnp.concatenate([rr.astype(BF), ri.astype(BF)], axis=0))
    cr[i] = f[:B]
    ci[i] = f[B:]


def cross(fr, fi, gr, gi):
    return fr * gr + fi * gi, fi * gr - fr * gi


def middle(b, gbuf, cr, ci, mg, sums):
    ln = lane((B, B))
    g = gbuf[b, 0:B, :].astype(F32)
    gs = pltpu.roll(g, 64, 1)
    gr = jnp.where(ln < 64, g, gs)
    gi = jnp.where(ln < 64, gs, g)
    re, im = cross(cr[b], ci[b], gr, gi)
    m = magnitude(re, im)
    cr[b], ci[b], mg[b] = re, im, m
    sums[pl.ds(b, 1), :] = jnp.sum(m, axis=0, keepdims=True)


def nyquist(cc, gbuf, r64, dc, ey, sums, mean, q64):
    first = pl.multiple_of(cc * 16, 16)
    col = jnp.where(cc == 0, r64[...], pltpu.roll(r64[...], B - 16, 1))
    f = dot(dc, jnp.concatenate([col.astype(BF), jnp.zeros((B, B), BF)], axis=0))
    z = jnp.zeros((48, B), F32)
    g = gbuf[pl.ds(first, 16), B : B + 16, :].astype(F32)
    gr, gi = g[:, 0, :], g[:, 1, :]
    gr = jnp.transpose(jnp.concatenate([gr, z, gr, z], axis=0))
    gi = jnp.transpose(jnp.concatenate([gi, z, gi, z], axis=0))
    re, im = cross(f[:B], f[B:], gr, gi)
    m = magnitude(re, im)
    m64 = jnp.sum(m, axis=0, keepdims=True)
    ln = lane((16, B))
    half = jnp.bitwise_and(ln, 63)
    diag = half == lax.broadcasted_iota(jnp.int32, (16, B), 0)
    s = sums[pl.ds(first, 16), :] * jnp.where(half == 0, 1.0, 2.0) + jnp.where(diag, m64, 0.0)
    s0 = jnp.sum(jnp.where(ln < 64, s, 0.0), axis=1, keepdims=True)
    s1 = jnp.sum(jnp.where(ln < 64, 0.0, s), axis=1, keepdims=True)
    mm = jnp.where(ln < 64, s0, s1) * (1.0 / (B * B)) + 1e-6
    mean[pl.ds(first, 16), :] = mm
    mrow = jnp.sum(jnp.where(diag, mm, 0.0), axis=0, keepdims=True)
    live = jnp.bitwise_and(lane((1, B)), 63) < 16
    inv = 1.0 / (m + jnp.where(live, mrow, 1.0))
    w = jnp.concatenate([(re * inv).astype(BF), (im * inv).astype(BF)], axis=0)
    q64[...] = dot(ey, w)[0:32]


def back(cc, yy, zt, n, spare, codes, cr, ci, mg, mean, q64, ey, ex, win, flat):
    i = cc * 16 + yy * 8 + zt
    b = block_of(i)
    inv = 1.0 / (mg[i] + mean[pl.ds(i, 1), :])
    w = jnp.concatenate([(cr[i] * inv).astype(BF), (ci[i] * inv).astype(BF)], axis=0)
    q = dot(ey, w)
    half = jnp.bitwise_and(lane((32, B)), 63)
    qi = jnp.where(half == 0, pltpu.roll(q64[...], jnp.bitwise_and(B - (yy * 8 + zt), B - 1), 1), q[32:64])
    win[spare] = dot(jnp.concatenate([q[0:32].astype(BF), qi.astype(BF)], axis=1), ex)
    for v in range(2):
        sy = jnp.right_shift(codes[v, 0, b], 4)
        sx = jnp.right_shift(codes[v, 1, b], 4)
        piece = win[spare, pl.ds(sy + 8, 16), :]
        piece = pltpu.roll(piece, jnp.bitwise_and(B - (8 + 32 * v) - sx, B - 1), 1)
        flat[pl.ds(n * B + v * 4 + yy * 2 + cc, 16, stride=8), :] = piece


def flatten(flat, n):
    ln = lane((8, B))
    tiles = []
    for t in range(2):
        out = None
        for k in range(8):
            a = t * 8 + k
            piece = flat[pl.ds(pl.multiple_of(n * B + a * 8, 8), 8), :]
            if k:
                piece = pltpu.roll(piece, 16 * k, 1)
            out = piece if out is None else jnp.where(ln >= 16 * k, piece, out)
        tiles.append(out)
    return jnp.concatenate(tiles, axis=1)


MESH = pl.DeviceIdType.MESH
ANY = pl.BlockSpec(memory_space=pltpu.HBM)
VM = pl.BlockSpec(memory_space=pltpu.VMEM)
SM = pl.BlockSpec(memory_space=pltpu.SMEM)
NEAR = (1, 7, 2, 6, 3, 5, 4)
ORDER = (4, 3, 5, 2, 6, 1, 7, 0)
GZ, GY, GS, SA, SY, SZ, CP, NSEM = 0, 8, 16, 32, 34, 34, 42, 50


def WARP_EVENTS(chain, z, y, send_a, await_a, zs):
    return dict(
        _1=send_a(0), _3=send_a(1), _5=z(1, 7), _6=chain(z(2, 6), y(0)), _7=chain(await_a(0), zs(4, 3)))


def FRONT_EVENTS(chain, z, y, send_a, await_a, zs):
    return dict(
        _0=chain(z(3, 5), zs(5, 2)), _1=chain(z(4), await_a(1), zs(6, 1)), _2=chain(y(1, 7), zs(7)), _3=y(2, 6),
        _5=y(3, 5), _7=y(4))


def kernel(codes, frames, y_h, dr_h, dc_h, ey_h, ex_h, ext_h, out_c, out_t,
           x, ext, extc, extr, y, dr, dc, ey, ex, g, r64, cr, ci, mg, sums, mean, q64, win, flat, sent,
           part, ra, sb, rb, sc, rc, rp, own, local, send, recv):
    tm = lax.axis_index("tm")
    z, yh, c, p = tm // 4, (tm // 2) % 2, tm % 2, lax.axis_index("plane")

    def at(zz, yy, cc, pp):
        return (zz * 4 + yy * 2 + cc, pp)

    up = [at((z + d) % 8, yh, c, p) for d in range(8)]
    across, sibling = at(z, 1 - yh, c, p), at(z, yh, 1 - c, p)
    peers = [at(z, yh, c, (p + d) % 8) for d in range(8)]

    def slot(cc, yy, zz):
        return cc * 16 + yy * 8 + zz

    def copy(src, dst, sem, dev):
        return pltpu.make_async_remote_copy(
            src_ref=src, dst_ref=dst, send_sem=send.at[sem], recv_sem=recv.at[sem],
            device_id=dev, device_id_type=MESH)

    def spectrum_copy(at_slot, sem, dev):
        return copy(g.at[at_slot], g.at[at_slot], sem, dev)

    loads = [pltpu.make_async_copy(a, b, local.at[n]) for n, (a, b) in enumerate(
        ((y_h.at[0, 0], y), (dr_h, dr), (dc_h, dc), (ext_h, ext),
         (frames.at[:, 0], x.at[:, 16:528, B:1152]), (ey_h, ey), (ex_h, ex)))]
    for cp in loads:
        cp.start()
    barrier = pltpu.get_barrier_semaphore()
    greeted = up[1:] + [across, sibling] + peers[1:]
    for dev in greeted:
        pl.semaphore_signal(barrier, inc=1, device_id=dev, device_id_type=MESH)
    x[:, 0:16, :] = jnp.zeros((2, 16, 1280), BF)
    x[:, 528:544, :] = jnp.zeros((2, 16, 1280), BF)
    x[:, 16:528, 0:B] = jnp.zeros((2, 512, B), BF)
    x[:, 16:528, 1152:1280] = jnp.zeros((2, 512, B), BF)
    r64[...] = jnp.zeros_like(r64)
    for cp in loads[:3]:
        cp.wait()
    mine = slot(c, yh, z)
    main, nyq = own_spectrum(y[...], dr[...], dc[...])
    g[mine, 0:B, :] = main
    g[mine, B : B + 16, :] = nyq
    pl.semaphore_wait(barrier, len(greeted))
    for d in NEAR:
        spectrum_copy(mine, GZ + d, up[d]).start()
    spectrum_copy(mine, GY, across).start()
    spectrum_copy(mine, GS, sibling).start()
    loads[3].wait()
    stage_tables(ext, extc, extr)
    for cp in loads[4:]:
        cp.wait()

    def z_arrived(d):
        s = slot(c, yh, (z + 8 - d) % 8)
        spectrum_copy(s, GZ + d, up[d]).wait_recv()
        spectrum_copy(s, GY + d, across).start()
        spectrum_copy(s, GS + d, sibling).start()

    def y_arrived(d):
        s = slot(c, 1 - yh, (z + 8 - d) % 8)
        spectrum_copy(s, GY + d, across).wait_recv()
        spectrum_copy(s, GS + 8 + d, sibling).start()

    def sibling_arrived(k):
        for d in range(8):
            s = slot(1 - c, yh if k == 0 else 1 - yh, (z + 8 - d) % 8)
            spectrum_copy(s, GS + 8 * k + d, sibling).wait_recv()

    def sum_a(n):
        return copy(part.at[pl.ds(8 * n, 8)], ra.at[pl.ds(8 * n, 8)], SA + n, sibling)

    def sum_z(d):
        return copy(sc.at[ORDER.index(d)], rc.at[d - 1], SZ + d, up[d])

    def sum_y():
        return copy(sb, rb, SY, across)

    def pair(d):
        n = ORDER.index(d)
        here, there = part[16 + 2 * n : 18 + 2 * n], ra[2 * n : 2 * n + 2]
        return here.astype(F32) + there.astype(F32)

    def send_z(ds):
        for d in ds:
            sc[ORDER.index(d)] = pair(d).astype(BF)
            sum_z(d).start()

    def slot_of(w):
        cc = jnp.where(w < 16, 1 - c, c)
        m = (w % 16) // 4
        d = jnp.where((w // 2) % 2 == 0, 4 + m, 3 - m)
        return cc * 16 + (w % 2) * 8 + (z + d) % 8

    def phase(step, order, **events):
        def group(n, _):
            for j in range(4):
                step((n if order else 7 - n) * 4 + j)
            for name, event in events.items():
                pl.when(n == int(name[1:]))(event)
            return 0

        lax.fori_loop(0, 8, group, 0)

    def z_arrivals(*ds):
        for d in ds:
            z_arrived(d)

    def y_arrivals(*ds):
        for d in ds:
            y_arrived(d)

    def warp_step(w):
        part[w] = warp_block(slot_of(w), codes, x, extc, extr).astype(BF)

    def z_event(*ds):
        return lambda: z_arrivals(*ds)

    def y_event(*ds):
        return lambda: y_arrivals(*ds)

    def chain(*events):
        def run():
            for event in events:
                event()
        return run

    def send_a(n):
        return lambda: sum_a(n).start()

    def z_sums(*ds):
        return lambda: send_z(ds)

    def await_a(n):
        return lambda: sum_a(n).wait_recv()

    phase(warp_step, True, **WARP_EVENTS(chain, z_event, y_event, send_a, await_a, z_sums))

    def front_step(w):
        front(slot_of(w), x, dr[...], dc[...], r64, cr, ci)

    phase(front_step, True, **FRONT_EVENTS(chain, z_event, y_event, send_a, await_a, z_sums))

    def window_copy(d):
        return copy(sent.at[d], rp.at[d - 1], CP + d, peers[d])

    def correlate(cc, last):
        def middle_group(n, _):
            if last:
                pl.when(n == 0)(lambda: sibling_arrived(0))
                pl.when(n == 2)(lambda: sibling_arrived(1))
            for j in range(4):
                middle(slot(cc, jnp.where(n < 2, yh, 1 - yh), (n % 2) * 4 + j), g, cr, ci, mg, sums)
            return 0

        lax.fori_loop(0, 4, middle_group, 0)
        nyquist(cc, g, r64, dc[...], ey[...], sums, mean, q64)

        def back_pair(h, _):
            for e in range(2):
                n = 2 * h + e
                zt = (p + 1 + n) % 8
                for yy in range(2):
                    back(cc, yy, zt, n, 2 * e + yy, codes, cr, ci, mg, mean, q64, ey[...], ex[...], win, flat)
                if last:
                    sent[(n + 1) % 8] = flatten(flat, n)
            if last:
                for d in range(1, 8):
                    pl.when(h == (d - 1) // 2)(lambda d=d: window_copy(d).start())
            return 0

        lax.fori_loop(0, 4, back_pair, 0)

    correlate(c, False)
    correlate(1 - c, True)
    for d in range(1, 8):
        sum_z(d).wait_recv()

    def summed(yy):
        total = part[30 + yy].astype(F32) + ra[14 + yy].astype(F32)
        for d in range(7):
            total = total + rc[d, yy].astype(F32)
        return total

    sb[...] = summed(1 - yh).astype(BF)
    sum_y().start()
    own[...] = summed(yh)
    for d in range(8):
        if d:
            spectrum_copy(mine, GZ + d, up[d]).wait_send()
            sum_z(d).wait_send()
        spectrum_copy(mine, GY + d, across).wait_send()
        spectrum_copy(mine, GS + d, sibling).wait_send()
        spectrum_copy(mine, GS + 8 + d, sibling).wait_send()
    sum_a(0).wait_send()
    sum_a(1).wait_send()
    for d in range(1, 8):
        window_copy(d).wait_recv()
    total = sent[0]
    for d in range(7):
        total = total + rp[d]
    out_c[0] = total[0:4]
    out_c[1] = total[4:8]
    sum_y().wait_recv()
    out_t[0, 0] = (own[...] + rb[...].astype(F32)) * (1.0 / 64)
    sum_y().wait_send()
    for d in range(1, 8):
        window_copy(d).wait_send()


def on_device(frames, template, codes):
    vm = pltpu.VMEM
    dma = pltpu.SemaphoreType.DMA
    return pl.pallas_call(
        kernel,
        out_shape=[jax.ShapeDtypeStruct((2, 4, 256), F32), jax.ShapeDtypeStruct((1, 1, B, B), F32)],
        in_specs=[SM] + [ANY] * 7,
        out_specs=[VM, VM],
        scratch_shapes=[
            vm((2, 544, 1280), BF), vm((16, 336, B), BF), vm((16, 272, B), F32), vm((32, 144, B), F32),
            vm((B, B), BF), vm((2 * B, 2 * B), BF), vm((2 * B, 2 * B), BF), vm((64, 2 * B), BF), vm((2 * B, B), BF),
            vm((NB, 144, B), BF), vm((B, B), F32),
            vm((NB, B, B), F32), vm((NB, B, B), F32), vm((NB, B, B), F32),
            vm((NB, B), F32), vm((NB, B), F32), vm((32, B), F32),
            vm((4, 32, B), F32), vm((8 * B, B), F32), vm((8, 8, 2 * B), F32),
            vm((NB, B, B), BF), vm((16, B, B), BF), vm((B, B), BF), vm((B, B), BF),
            vm((8, 2, B, B), BF), vm((7, 2, B, B), BF), vm((7, 8, 2 * B), F32), vm((B, B), F32),
            dma((7,)), dma((NSEM,)), dma((NSEM,)),
        ],
        compiler_params=pltpu.CompilerParams(
            collective_id=0, has_side_effects=True, vmem_limit_bytes=67043328),
    )(codes, frames, template, *tables())


def solution(mesh):
    in_specs = (P("tm", "plane", None, None), P("tm", "plane", None, None), P("tm", None, None))
    out_specs = (P("tm", "plane", None), P("tm", "plane", None, None))
    return jax.shard_map(on_device, mesh=mesh, in_specs=in_specs, out_specs=out_specs, check_vma=False)
```

```python
import numpy as np
import jax
import jax.numpy as jnp
from jax import lax
from jax.experimental import pallas as pl
from jax.experimental.pallas import tpu as pltpu
from jax.sharding import PartitionSpec as P

B = 128
NB = 32
BX = 8
F32 = jnp.float32
BF = jnp.bfloat16


def tables():
    n = np.arange(B)
    ang = 2 * np.pi * ((n[:, None] * n[None, :]) % B) / B
    cos, sin = np.cos(ang), -np.sin(ang)
    h = B // 2
    dr = np.zeros((2 * B, 2 * B))
    for v in range(2):
        dr[v * B : v * B + B, v * h : v * h + h] = cos[:, :h]
        dr[v * B : v * B + B, B + v * h : B + v * h + h] = sin[:, :h]
        dr[v * B : v * B + B, B + v * h] = cos[:, h]
    dc = np.block([[cos, -sin], [sin, cos]])
    lag = np.arange(32) - 16
    ay = 2 * np.pi * ((lag[:, None] * n[None, :]) % B) / B
    ey = np.block([[np.cos(ay), -np.sin(ay)], [np.sin(ay), np.cos(ay)]])
    ax = 2 * np.pi * ((n[:h, None] * lag[None, :]) % B) / B
    w = np.where(n[:h] == 0, 1.0, 2.0)[:, None] / B
    ex = np.zeros((2 * B, B))
    for v in range(2):
        ex[v * h : v * h + h, v * 32 : v * 32 + 32] = w * np.cos(ax)
        ex[B + v * h : B + v * h + h, v * 32 : v * 32 + 32] = -w * np.sin(ax)
        ex[B + v * h, v * 32 : v * 32 + 32] = np.where(lag % 2 == 0, 1.0, -1.0) / B
    i = np.arange(8) - 3
    t = i[None, :] - np.arange(16)[:, None] / 16
    raw = np.sinc(t) * np.sinc(t / 4)
    tap = raw / raw.sum(-1, keepdims=True)
    tap = np.concatenate([tap, np.zeros((16, 248))], 1)
    nn = np.arange(272)
    extc = tap[:, (nn[:, None] - n[None, :] - 5) % 256]
    nr, q = np.arange(144), np.arange(256)
    extr = tap[:, (q[None, :] - nr[:, None] - 5) % 256]
    ext = np.concatenate([extc[:, :144], extc[:, 256:272], extr[..., :B], extr[:, 112:144, B:]], 1)
    return [np.asarray(x, np.float32).astype(BF) for x in (dr, dc, ey, ex, ext)]


def dot(a, b):
    return jnp.dot(a, b, preferred_element_type=F32)


def lane(shape):
    return lax.broadcasted_iota(jnp.int32, shape, len(shape) - 1)


def row_stage(x0, x1, dr):
    return dot(jnp.concatenate([x0, x1], axis=1), dr)


def own_spectrum(y, dr, dc):
    r = row_stage(y, y, dr)
    rr, ri = r[:, :B], r[:, B:]
    ln = lane((B, B))
    rr2 = jnp.where(ln == 64, ri, rr)
    ri2 = jnp.where((ln == 64) | (ln == 0), 0.0, ri)
    f = dot(dc, jnp.concatenate([rr2, ri2], axis=0).astype(BF))
    fr, fi = f[:B], f[B:]
    main = jnp.where(ln < 64, fr, fi)
    main = jnp.where(ln == 64, pltpu.roll(fi, 64, 1), main)
    nr = jnp.transpose(fr)[64:72]
    ni = jnp.transpose(fi)[64:72]
    row = lax.broadcasted_iota(jnp.int32, (16, B), 0)
    nyq = jnp.where(row == 0, jnp.concatenate([nr, nr], axis=0),
                    pltpu.roll(jnp.concatenate([ni, ni], axis=0), 1, 0))
    return main.astype(BF), nyq.astype(BF)


def stage_tables(ext, extc, extr):
    zero = jnp.zeros((112, B), F32)

    def body(f, _):
        extc[f, 0:144] = ext[f, 0:144].astype(F32)
        extc[f, 144:256] = zero
        extc[f, 256:272] = ext[f, 144:160].astype(F32)
        extr[f] = ext[f, 160:304].astype(F32)
        extr[16 + f, 0:112] = zero
        extr[16 + f, 112:144] = ext[f, 304:336].astype(F32)
        return 0

    lax.fori_loop(0, 16, body, 0)


def block_of(i):
    return (i % 8) * 4 + ((i // 8) % 2) * 2 + i // 16


def warp_block(i, codes, x, extc, extr):
    b = block_of(i)
    by, bx = b // BX, b % BX
    row0 = pl.multiple_of(by * B, B)
    col0 = pl.multiple_of(bx * B, B)
    ln = lane((160, B))
    zero = jnp.zeros((96, B), BF)
    total = None
    for v in range(2):
        cy, cx = codes[v, 0, b], codes[v, 1, b]
        sy, fy = jnp.right_shift(cy, 4), jnp.bitwise_and(cy, 15)
        sx, fx = jnp.right_shift(cx, 4), jnp.bitwise_and(cx, 15)
        acol = extc[fx, pl.ds(8 - sx, 256), :].astype(BF)
        arow = jnp.concatenate([extr[fy, pl.ds(8 + sy, 128), :].astype(BF), extr[16 + fy, pl.ds(8 + sy, 128), :].astype(BF)], axis=1)
        left = x[v, pl.ds(row0, 160), pl.ds(col0, B)]
        main = x[v, pl.ds(row0, 160), pl.ds(col0 + B, B)]
        right = x[v, pl.ds(row0, 160), pl.ds(col0 + 2 * B, B)]
        halo = jnp.where(ln < 64, right, left)
        t = dot(jnp.concatenate([main, halo], axis=1), acol).astype(BF)
        o = dot(arow, jnp.concatenate([t, zero], axis=0))
        total = o if total is None else total + o
    return total


def magnitude(re, im):
    sq = re * re + im * im
    return sq * lax.rsqrt(jnp.maximum(sq, 1e-37))


def front(i, x, dr, dc, r64, cr, ci):
    b = block_of(i)
    by, bx = b // BX, b % BX
    row0 = pl.multiple_of(by * B + 16, 16)
    col0 = pl.multiple_of(bx * B + B, B)
    ln = lane((B, B))
    r = row_stage(x[0, pl.ds(row0, B), pl.ds(col0, B)], x[1, pl.ds(row0, B), pl.ds(col0, B)], dr)
    rr, ri = r[:, :B], r[:, B:]
    half = jnp.bitwise_and(ln, 63)
    r64[...] = jnp.where(half == i, pltpu.roll(ri, i, 1), r64[...])
    ri = jnp.where(half == 0, 0.0, ri)
    f = dot(dc, jnp.concatenate([rr.astype(BF), ri.astype(BF)], axis=0))
    cr[i] = f[:B]
    ci[i] = f[B:]


def cross(fr, fi, gr, gi):
    return fr * gr + fi * gi, fi * gr - fr * gi


def middle(b, gbuf, cr, ci, mg, sums):
    ln = lane((B, B))
    g = gbuf[b, 0:B, :].astype(F32)
    gs = pltpu.roll(g, 64, 1)
    gr = jnp.where(ln < 64, g, gs)
    gi = jnp.where(ln < 64, gs, g)
    re, im = cross(cr[b], ci[b], gr, gi)
    m = magnitude(re, im)
    cr[b], ci[b], mg[b] = re, im, m
    sums[pl.ds(b, 1), :] = jnp.sum(m, axis=0, keepdims=True)


def nyquist(cc, gbuf, r64, dc, ey, sums, mean, q64):
    first = pl.multiple_of(cc * 16, 16)
    col = jnp.where(cc == 0, r64[...], pltpu.roll(r64[...], B - 16, 1))
    f = dot(dc, jnp.concatenate([col.astype(BF), jnp.zeros((B, B), BF)], axis=0))
    z = jnp.zeros((48, B), F32)
    g = gbuf[pl.ds(first, 16), B : B + 16, :].astype(F32)
    gr, gi = g[:, 0, :], g[:, 1, :]
    gr = jnp.transpose(jnp.concatenate([gr, z, gr, z], axis=0))
    gi = jnp.transpose(jnp.concatenate([gi, z, gi, z], axis=0))
    re, im = cross(f[:B], f[B:], gr, gi)
    m = magnitude(re, im)
    m64 = jnp.sum(m, axis=0, keepdims=True)
    ln = lane((16, B))
    half = jnp.bitwise_and(ln, 63)
    diag = half == lax.broadcasted_iota(jnp.int32, (16, B), 0)
    s = sums[pl.ds(first, 16), :] * jnp.where(half == 0, 1.0, 2.0) + jnp.where(diag, m64, 0.0)
    s0 = jnp.sum(jnp.where(ln < 64, s, 0.0), axis=1, keepdims=True)
    s1 = jnp.sum(jnp.where(ln < 64, 0.0, s), axis=1, keepdims=True)
    mm = jnp.where(ln < 64, s0, s1) * (1.0 / (B * B)) + 1e-6
    mean[pl.ds(first, 16), :] = mm
    mrow = jnp.sum(jnp.where(diag, mm, 0.0), axis=0, keepdims=True)
    live = jnp.bitwise_and(lane((1, B)), 63) < 16
    inv = 1.0 / (m + jnp.where(live, mrow, 1.0))
    w = jnp.concatenate([(re * inv).astype(BF), (im * inv).astype(BF)], axis=0)
    q64[...] = dot(ey, w)[0:32]


def back(cc, yy, zt, n, spare, codes, cr, ci, mg, mean, q64, ey, ex, win, flat):
    i = cc * 16 + yy * 8 + zt
    b = block_of(i)
    inv = 1.0 / (mg[i] + mean[pl.ds(i, 1), :])
    w = jnp.concatenate([(cr[i] * inv).astype(BF), (ci[i] * inv).astype(BF)], axis=0)
    q = dot(ey, w)
    half = jnp.bitwise_and(lane((32, B)), 63)
    qi = jnp.where(half == 0, pltpu.roll(q64[...], jnp.bitwise_and(B - (yy * 8 + zt), B - 1), 1), q[32:64])
    win[spare] = dot(jnp.concatenate([q[0:32].astype(BF), qi.astype(BF)], axis=1), ex)
    for v in range(2):
        sy = jnp.right_shift(codes[v, 0, b], 4)
        sx = jnp.right_shift(codes[v, 1, b], 4)
        piece = win[spare, pl.ds(sy + 8, 16), :]
        piece = pltpu.roll(piece, jnp.bitwise_and(B - (8 + 32 * v) - sx, B - 1), 1)
        flat[pl.ds(n * B + v * 4 + yy * 2 + cc, 16, stride=8), :] = piece


def flatten(flat, n):
    ln = lane((8, B))
    tiles = []
    for t in range(2):
        out = None
        for k in range(8):
            a = t * 8 + k
            piece = flat[pl.ds(pl.multiple_of(n * B + a * 8, 8), 8), :]
            if k:
                piece = pltpu.roll(piece, 16 * k, 1)
            out = piece if out is None else jnp.where(ln >= 16 * k, piece, out)
        tiles.append(out)
    return jnp.concatenate(tiles, axis=1)


MESH = pl.DeviceIdType.MESH
ANY = pl.BlockSpec(memory_space=pltpu.HBM)
VM = pl.BlockSpec(memory_space=pltpu.VMEM)
SM = pl.BlockSpec(memory_space=pltpu.SMEM)
NEAR = (1, 7, 2, 6, 3, 5, 4)
ORDER = (4, 3, 5, 2, 6, 1, 7, 0)
GZ, GY, GS, SA, SY, SZ, CP, NSEM = 0, 8, 16, 32, 34, 34, 42, 50


def WARP_EVENTS(chain, z, y, send_a, await_a, zs):
    return dict(_1=send_a(0), _3=send_a(1), _5=chain(await_a(0), zs(4, 3)), _6=chain(z(1, 7), y(0), zs(5, 2)), _7=chain(z(2, 6), await_a(1), zs(6, 1)))


def FRONT_EVENTS(chain, z, y, send_a, await_a, zs):
    return dict(_0=zs(7), _1=z(3, 5), _2=z(4), _3=y(1, 7), _4=y(2, 6), _6=y(3, 5), _7=y(4))


def kernel(codes, frames, y_h, dr_h, dc_h, ey_h, ex_h, ext_h, out_c, out_t,
           x, ext, extc, extr, y, dr, dc, ey, ex, g, r64, cr, ci, mg, sums, mean, q64, win, flat, sent,
           part, ra, sb, rb, sc, rc, rp, own, local, send, recv):
    tm = lax.axis_index("tm")
    z, yh, c, p = tm // 4, (tm // 2) % 2, tm % 2, lax.axis_index("plane")

    def at(zz, yy, cc, pp):
        return (zz * 4 + yy * 2 + cc, pp)

    up = [at((z + d) % 8, yh, c, p) for d in range(8)]
    across, sibling = at(z, 1 - yh, c, p), at(z, yh, 1 - c, p)
    peers = [at(z, yh, c, (p + d) % 8) for d in range(8)]

    def slot(cc, yy, zz):
        return cc * 16 + yy * 8 + zz

    def copy(src, dst, sem, dev):
        return pltpu.make_async_remote_copy(
            src_ref=src, dst_ref=dst, send_sem=send.at[sem], recv_sem=recv.at[sem],
            device_id=dev, device_id_type=MESH)

    def spectrum_copy(at_slot, sem, dev):
        return copy(g.at[at_slot], g.at[at_slot], sem, dev)

    loads = [pltpu.make_async_copy(a, b, local.at[n]) for n, (a, b) in enumerate(
        ((y_h.at[0, 0], y), (dr_h, dr), (dc_h, dc), (ext_h, ext),
         (frames.at[:, 0], x.at[:, 16:528, B:1152]), (ey_h, ey), (ex_h, ex)))]
    for cp in loads:
        cp.start()
    barrier = pltpu.get_barrier_semaphore()
    greeted = up[1:] + [across, sibling] + peers[1:]
    for dev in greeted:
        pl.semaphore_signal(barrier, inc=1, device_id=dev, device_id_type=MESH)
    x[:, 0:16, :] = jnp.zeros((2, 16, 1280), BF)
    x[:, 528:544, :] = jnp.zeros((2, 16, 1280), BF)
    x[:, 16:528, 0:B] = jnp.zeros((2, 512, B), BF)
    x[:, 16:528, 1152:1280] = jnp.zeros((2, 512, B), BF)
    r64[...] = jnp.zeros_like(r64)
    for cp in loads[:3]:
        cp.wait()
    mine = slot(c, yh, z)
    main, nyq = own_spectrum(y[...], dr[...], dc[...])
    g[mine, 0:B, :] = main
    g[mine, B : B + 16, :] = nyq
    pl.semaphore_wait(barrier, len(greeted))
    for d in NEAR:
        spectrum_copy(mine, GZ + d, up[d]).start()
    spectrum_copy(mine, GY, across).start()
    spectrum_copy(mine, GS, sibling).start()
    loads[3].wait()
    stage_tables(ext, extc, extr)
    for cp in loads[4:]:
        cp.wait()

    def z_arrived(d):
        s = slot(c, yh, (z + 8 - d) % 8)
        spectrum_copy(s, GZ + d, up[d]).wait_recv()
        spectrum_copy(s, GY + d, across).start()
        spectrum_copy(s, GS + d, sibling).start()

    def y_arrived(d):
        s = slot(c, 1 - yh, (z + 8 - d) % 8)
        spectrum_copy(s, GY + d, across).wait_recv()
        spectrum_copy(s, GS + 8 + d, sibling).start()

    def sibling_arrived(k):
        for d in range(8):
            s = slot(1 - c, yh if k == 0 else 1 - yh, (z + 8 - d) % 8)
            spectrum_copy(s, GS + 8 * k + d, sibling).wait_recv()

    def sum_a(n):
        return copy(part.at[pl.ds(8 * n, 8)], ra.at[pl.ds(8 * n, 8)], SA + n, sibling)

    def sum_z(d):
        return copy(sc.at[ORDER.index(d)], rc.at[d - 1], SZ + d, up[d])

    def sum_y():
        return copy(sb, rb, SY, across)

    def pair(d):
        n = ORDER.index(d)
        here, there = part[16 + 2 * n : 18 + 2 * n], ra[2 * n : 2 * n + 2]
        return here.astype(F32) + there.astype(F32)

    def send_z(ds):
        for d in ds:
            sc[ORDER.index(d)] = pair(d).astype(BF)
            sum_z(d).start()

    def slot_of(w):
        cc = jnp.where(w < 16, 1 - c, c)
        m = (w % 16) // 4
        d = jnp.where((w // 2) % 2 == 0, 4 + m, 3 - m)
        return cc * 16 + (w % 2) * 8 + (z + d) % 8

    def phase(step, order, **events):
        def group(n, _):
            for j in range(4):
                step((n if order else 7 - n) * 4 + j)
            for name, event in events.items():
                pl.when(n == int(name[1:]))(event)
            return 0

        lax.fori_loop(0, 8, group, 0)

    def z_arrivals(*ds):
        for d in ds:
            z_arrived(d)

    def y_arrivals(*ds):
        for d in ds:
            y_arrived(d)

    def warp_step(w):
        part[w] = warp_block(slot_of(w), codes, x, extc, extr).astype(BF)

    def z_event(*ds):
        return lambda: z_arrivals(*ds)

    def y_event(*ds):
        return lambda: y_arrivals(*ds)

    def chain(*events):
        def run():
            for event in events:
                event()
        return run

    def send_a(n):
        return lambda: sum_a(n).start()

    def z_sums(*ds):
        return lambda: send_z(ds)

    def await_a(n):
        return lambda: sum_a(n).wait_recv()

    phase(warp_step, True, **WARP_EVENTS(chain, z_event, y_event, send_a, await_a, z_sums))

    def front_step(w):
        front(slot_of(w), x, dr[...], dc[...], r64, cr, ci)

    phase(front_step, True, **FRONT_EVENTS(chain, z_event, y_event, send_a, await_a, z_sums))

    def window_copy(d):
        return copy(sent.at[d], rp.at[d - 1], CP + d, peers[d])

    def correlate(cc, last):
        def middle_group(n, _):
            if last:
                pl.when(n == 0)(lambda: sibling_arrived(0))
                pl.when(n == 2)(lambda: sibling_arrived(1))
            for j in range(4):
                middle(slot(cc, jnp.where(n < 2, yh, 1 - yh), (n % 2) * 4 + j), g, cr, ci, mg, sums)
            return 0

        lax.fori_loop(0, 4, middle_group, 0)
        nyquist(cc, g, r64, dc[...], ey[...], sums, mean, q64)

        def back_groups(h, _):
            for e in range(4):
                n = 4 * h + e
                zt = (p + 1 + n) % 8
                for yy in range(2):
                    back(cc, yy, zt, n, 2 * e + yy, codes, cr, ci, mg, mean, q64, ey[...], ex[...], win, flat)
                if last:
                    sent[(n + 1) % 8] = flatten(flat, n)
            if last:
                for d in range(1, 8):
                    pl.when(h == (d - 1) // 4)(lambda d=d: window_copy(d).start())
            return 0

        lax.fori_loop(0, 2, back_groups, 0)

    correlate(c, False)
    correlate(1 - c, True)
    for d in range(1, 8):
        sum_z(d).wait_recv()

    def summed(yy):
        total = part[30 + yy].astype(F32) + ra[14 + yy].astype(F32)
        for d in range(7):
            total = total + rc[d, yy].astype(F32)
        return total

    sb[...] = summed(1 - yh).astype(BF)
    sum_y().start()
    own[...] = summed(yh)
    for d in range(8):
        if d:
            spectrum_copy(mine, GZ + d, up[d]).wait_send()
            sum_z(d).wait_send()
        spectrum_copy(mine, GY + d, across).wait_send()
        spectrum_copy(mine, GS + d, sibling).wait_send()
        spectrum_copy(mine, GS + 8 + d, sibling).wait_send()
    sum_a(0).wait_send()
    sum_a(1).wait_send()
    for d in range(1, 8):
        window_copy(d).wait_recv()
    total = sent[0]
    for d in range(7):
        total = total + rp[d]
    out_c[0] = total[0:4]
    out_c[1] = total[4:8]
    sum_y().wait_recv()
    out_t[0, 0] = (own[...] + rb[...].astype(F32)) * (1.0 / 64)
    sum_y().wait_send()
    for d in range(1, 8):
        window_copy(d).wait_send()


def on_device(frames, template, codes):
    vm = pltpu.VMEM
    dma = pltpu.SemaphoreType.DMA
    return pl.pallas_call(
        kernel,
        out_shape=[jax.ShapeDtypeStruct((2, 4, 256), F32), jax.ShapeDtypeStruct((1, 1, B, B), F32)],
        in_specs=[SM] + [ANY] * 7,
        out_specs=[VM, VM],
        scratch_shapes=[
            vm((2, 544, 1280), BF), vm((16, 336, B), BF), vm((16, 272, B), F32), vm((32, 144, B), F32),
            vm((B, B), BF), vm((2 * B, 2 * B), BF), vm((2 * B, 2 * B), BF), vm((64, 2 * B), BF), vm((2 * B, B), BF),
            vm((NB, 144, B), BF), vm((B, B), F32),
            vm((NB, B, B), F32), vm((NB, B, B), F32), vm((NB, B, B), F32),
            vm((NB, B), F32), vm((NB, B), F32), vm((32, B), F32),
            vm((8, 32, B), F32), vm((8 * B, B), F32), vm((8, 8, 2 * B), F32),
            vm((NB, B, B), BF), vm((16, B, B), BF), vm((B, B), BF), vm((B, B), BF),
            vm((8, 2, B, B), BF), vm((7, 2, B, B), BF), vm((7, 8, 2 * B), F32), vm((B, B), F32),
            dma((7,)), dma((NSEM,)), dma((NSEM,)),
        ],
        compiler_params=pltpu.CompilerParams(
            collective_id=0, has_side_effects=True, vmem_limit_bytes=67043328),
    )(codes, frames, template, *tables())


def solution(mesh):
    in_specs = (P("tm", "plane", None, None), P("tm", "plane", None, None), P("tm", None, None))
    out_specs = (P("tm", "plane", None), P("tm", "plane", None, None))
    return jax.shard_map(on_device, mesh=mesh, in_specs=in_specs, out_specs=out_specs, check_vma=False)
```

```python
import numpy as np
import jax
import jax.numpy as jnp
from jax import lax
from jax.experimental import pallas as pl
from jax.experimental.pallas import tpu as pltpu
from jax.sharding import PartitionSpec as P

B = 128
NB = 32
BX = 8
F32 = jnp.float32
BF = jnp.bfloat16


def tables():
    n = np.arange(B)
    ang = 2 * np.pi * ((n[:, None] * n[None, :]) % B) / B
    cos, sin = np.cos(ang), -np.sin(ang)
    h = B // 2
    dr = np.zeros((2 * B, 2 * B))
    for v in range(2):
        dr[v * B : v * B + B, v * h : v * h + h] = cos[:, :h]
        dr[v * B : v * B + B, B + v * h : B + v * h + h] = sin[:, :h]
        dr[v * B : v * B + B, B + v * h] = cos[:, h]
    dc = np.block([[cos, -sin], [sin, cos]])
    lag = np.arange(32) - 16
    ay = 2 * np.pi * ((lag[:, None] * n[None, :]) % B) / B
    ey = np.block([[np.cos(ay), -np.sin(ay)], [np.sin(ay), np.cos(ay)]])
    ax = 2 * np.pi * ((n[:h, None] * lag[None, :]) % B) / B
    w = np.where(n[:h] == 0, 1.0, 2.0)[:, None] / B
    ex = np.zeros((2 * B, B))
    for v in range(2):
        ex[v * h : v * h + h, v * 32 : v * 32 + 32] = w * np.cos(ax)
        ex[B + v * h : B + v * h + h, v * 32 : v * 32 + 32] = -w * np.sin(ax)
        ex[B + v * h, v * 32 : v * 32 + 32] = np.where(lag % 2 == 0, 1.0, -1.0) / B
    i = np.arange(8) - 3
    t = i[None, :] - np.arange(16)[:, None] / 16
    raw = np.sinc(t) * np.sinc(t / 4)
    tap = raw / raw.sum(-1, keepdims=True)
    tap = np.concatenate([tap, np.zeros((16, 248))], 1)
    nn = np.arange(272)
    extc = tap[:, (nn[:, None] - n[None, :] - 5) % 256]
    nr, q = np.arange(144), np.arange(256)
    extr = tap[:, (q[None, :] - nr[:, None] - 5) % 256]
    ext = np.concatenate([extc[:, :144], extc[:, 256:272], extr[..., :B], extr[:, 112:144, B:]], 1)
    return [np.asarray(x, np.float32).astype(BF) for x in (dr, dc, ey, ex, ext)]


def dot(a, b):
    return jnp.dot(a, b, preferred_element_type=F32)


def lane(shape):
    return lax.broadcasted_iota(jnp.int32, shape, len(shape) - 1)


def row_stage(x0, x1, dr):
    return dot(jnp.concatenate([x0, x1], axis=1), dr)


def own_spectrum(y, dr, dc):
    r = row_stage(y, y, dr)
    rr, ri = r[:, :B], r[:, B:]
    ln = lane((B, B))
    rr2 = jnp.where(ln == 64, ri, rr)
    ri2 = jnp.where((ln == 64) | (ln == 0), 0.0, ri)
    f = dot(dc, jnp.concatenate([rr2, ri2], axis=0).astype(BF))
    fr, fi = f[:B], f[B:]
    main = jnp.where(ln < 64, fr, fi)
    main = jnp.where(ln == 64, pltpu.roll(fi, 64, 1), main)
    nr = jnp.transpose(fr)[64:72]
    ni = jnp.transpose(fi)[64:72]
    row = lax.broadcasted_iota(jnp.int32, (16, B), 0)
    nyq = jnp.where(row == 0, jnp.concatenate([nr, nr], axis=0),
                    pltpu.roll(jnp.concatenate([ni, ni], axis=0), 1, 0))
    return main.astype(BF), nyq.astype(BF)


def stage_tables(ext, extc, extr):
    zero = jnp.zeros((112, B), F32)

    def body(f, _):
        extc[f, 0:144] = ext[f, 0:144].astype(F32)
        extc[f, 144:256] = zero
        extc[f, 256:272] = ext[f, 144:160].astype(F32)
        extr[f] = ext[f, 160:304].astype(F32)
        extr[16 + f, 0:112] = zero
        extr[16 + f, 112:144] = ext[f, 304:336].astype(F32)
        return 0

    lax.fori_loop(0, 16, body, 0)


def block_of(i):
    return (i % 8) * 4 + ((i // 8) % 2) * 2 + i // 16


def warp_block(i, codes, x, extc, extr):
    b = block_of(i)
    by, bx = b // BX, b % BX
    row0 = pl.multiple_of(by * B, B)
    col0 = pl.multiple_of(bx * B, B)
    ln = lane((160, B))
    zero = jnp.zeros((96, B), BF)
    total = None
    for v in range(2):
        cy, cx = codes[v, 0, b], codes[v, 1, b]
        sy, fy = jnp.right_shift(cy, 4), jnp.bitwise_and(cy, 15)
        sx, fx = jnp.right_shift(cx, 4), jnp.bitwise_and(cx, 15)
        acol = extc[fx, pl.ds(8 - sx, 256), :].astype(BF)
        arow = jnp.concatenate([extr[fy, pl.ds(8 + sy, 128), :].astype(BF), extr[16 + fy, pl.ds(8 + sy, 128), :].astype(BF)], axis=1)
        left = x[v, pl.ds(row0, 160), pl.ds(col0, B)]
        main = x[v, pl.ds(row0, 160), pl.ds(col0 + B, B)]
        right = x[v, pl.ds(row0, 160), pl.ds(col0 + 2 * B, B)]
        halo = jnp.where(ln < 64, right, left)
        t = dot(jnp.concatenate([main, halo], axis=1), acol).astype(BF)
        o = dot(arow, jnp.concatenate([t, zero], axis=0))
        total = o if total is None else total + o
    return total


def magnitude(re, im):
    sq = re * re + im * im
    return sq * lax.rsqrt(jnp.maximum(sq, 1e-37))


def front(i, x, dr, dc, r64, cr, ci):
    b = block_of(i)
    by, bx = b // BX, b % BX
    row0 = pl.multiple_of(by * B + 16, 16)
    col0 = pl.multiple_of(bx * B + B, B)
    ln = lane((B, B))
    r = row_stage(x[0, pl.ds(row0, B), pl.ds(col0, B)], x[1, pl.ds(row0, B), pl.ds(col0, B)], dr)
    rr, ri = r[:, :B], r[:, B:]
    half = jnp.bitwise_and(ln, 63)
    r64[...] = jnp.where(half == i, pltpu.roll(ri, i, 1), r64[...])
    ri = jnp.where(half == 0, 0.0, ri)
    f = dot(dc, jnp.concatenate([rr.astype(BF), ri.astype(BF)], axis=0))
    cr[i] = f[:B]
    ci[i] = f[B:]


def cross(fr, fi, gr, gi):
    return fr * gr + fi * gi, fi * gr - fr * gi


def middle(b, gbuf, cr, ci, mg, sums):
    ln = lane((B, B))
    g = gbuf[b, 0:B, :].astype(F32)
    gs = pltpu.roll(g, 64, 1)
    gr = jnp.where(ln < 64, g, gs)
    gi = jnp.where(ln < 64, gs, g)
    re, im = cross(cr[b], ci[b], gr, gi)
    m = magnitude(re, im)
    cr[b], ci[b], mg[b] = re, im, m
    sums[pl.ds(b, 1), :] = jnp.sum(m, axis=0, keepdims=True)


def nyquist(cc, gbuf, r64, dc, ey, sums, mean, q64):
    first = pl.multiple_of(cc * 16, 16)
    col = jnp.where(cc == 0, r64[...], pltpu.roll(r64[...], B - 16, 1))
    f = dot(dc, jnp.concatenate([col.astype(BF), jnp.zeros((B, B), BF)], axis=0))
    z = jnp.zeros((48, B), F32)
    g = gbuf[pl.ds(first, 16), B : B + 16, :].astype(F32)
    gr, gi = g[:, 0, :], g[:, 1, :]
    gr = jnp.transpose(jnp.concatenate([gr, z, gr, z], axis=0))
    gi = jnp.transpose(jnp.concatenate([gi, z, gi, z], axis=0))
    re, im = cross(f[:B], f[B:], gr, gi)
    m = magnitude(re, im)
    m64 = jnp.sum(m, axis=0, keepdims=True)
    ln = lane((16, B))
    half = jnp.bitwise_and(ln, 63)
    diag = half == lax.broadcasted_iota(jnp.int32, (16, B), 0)
    s = sums[pl.ds(first, 16), :] * jnp.where(half == 0, 1.0, 2.0) + jnp.where(diag, m64, 0.0)
    s0 = jnp.sum(jnp.where(ln < 64, s, 0.0), axis=1, keepdims=True)
    s1 = jnp.sum(jnp.where(ln < 64, 0.0, s), axis=1, keepdims=True)
    mm = jnp.where(ln < 64, s0, s1) * (1.0 / (B * B)) + 1e-6
    mean[pl.ds(first, 16), :] = mm
    mrow = jnp.sum(jnp.where(diag, mm, 0.0), axis=0, keepdims=True)
    live = jnp.bitwise_and(lane((1, B)), 63) < 16
    inv = 1.0 / (m + jnp.where(live, mrow, 1.0))
    w = jnp.concatenate([(re * inv).astype(BF), (im * inv).astype(BF)], axis=0)
    q64[...] = dot(ey, w)[0:32]


def back(cc, yy, zt, n, spare, codes, cr, ci, mg, mean, q64, ey, ex, win, flat):
    i = cc * 16 + yy * 8 + zt
    b = block_of(i)
    inv = 1.0 / (mg[i] + mean[pl.ds(i, 1), :])
    w = jnp.concatenate([(cr[i] * inv).astype(BF), (ci[i] * inv).astype(BF)], axis=0)
    q = dot(ey, w)
    half = jnp.bitwise_and(lane((32, B)), 63)
    qi = jnp.where(half == 0, pltpu.roll(q64[...], jnp.bitwise_and(B - (yy * 8 + zt), B - 1), 1), q[32:64])
    win[spare] = dot(jnp.concatenate([q[0:32].astype(BF), qi.astype(BF)], axis=1), ex)
    for v in range(2):
        sy = jnp.right_shift(codes[v, 0, b], 4)
        sx = jnp.right_shift(codes[v, 1, b], 4)
        piece = win[spare, pl.ds(sy + 8, 16), :]
        piece = pltpu.roll(piece, jnp.bitwise_and(B - (8 + 32 * v) - sx, B - 1), 1)
        flat[pl.ds(n * B + v * 4 + yy * 2 + cc, 16, stride=8), :] = piece


def flatten(flat, n):
    ln = lane((8, B))
    tiles = []
    for t in range(2):
        out = None
        for k in range(8):
            a = t * 8 + k
            piece = flat[pl.ds(pl.multiple_of(n * B + a * 8, 8), 8), :]
            if k:
                piece = pltpu.roll(piece, 16 * k, 1)
            out = piece if out is None else jnp.where(ln >= 16 * k, piece, out)
        tiles.append(out)
    return jnp.concatenate(tiles, axis=1)


MESH = pl.DeviceIdType.MESH
ANY = pl.BlockSpec(memory_space=pltpu.HBM)
VM = pl.BlockSpec(memory_space=pltpu.VMEM)
SM = pl.BlockSpec(memory_space=pltpu.SMEM)
NEAR = (1, 7, 2, 6, 3, 5, 4)
ORDER = (4, 3, 5, 2, 6, 1, 7, 0)
GZ, GY, GS, SA, SY, SZ, CP, NSEM = 0, 8, 16, 32, 34, 34, 42, 50


def WARP_EVENTS(chain, z, y, send_a, await_a, zs):
    return dict(_1=send_a(0), _3=send_a(1), _5=chain(await_a(0), zs(4, 3)), _6=chain(z(1, 7), y(0), zs(5, 2)), _7=chain(z(2, 6), await_a(1), zs(6, 1)))


def FRONT_EVENTS(chain, z, y, send_a, await_a, zs):
    return dict(_0=zs(7), _1=z(3, 5), _2=z(4), _3=y(1, 7), _4=y(2, 6), _6=y(3, 5), _7=y(4))


def kernel(codes, frames, y_h, dr_h, dc_h, ey_h, ex_h, ext_h, out_c, out_t,
           x, ext, extc, extr, y, dr, dc, ey, ex, g, r64, cr, ci, mg, sums, mean, q64, win, flat, sent,
           part, ra, sb, rb, sc, rc, rp, own, local, send, recv):
    tm = lax.axis_index("tm")
    z, yh, c, p = tm // 4, (tm // 2) % 2, tm % 2, lax.axis_index("plane")

    def at(zz, yy, cc, pp):
        return (zz * 4 + yy * 2 + cc, pp)

    up = [at((z + d) % 8, yh, c, p) for d in range(8)]
    across, sibling = at(z, 1 - yh, c, p), at(z, yh, 1 - c, p)
    peers = [at(z, yh, c, (p + d) % 8) for d in range(8)]

    def slot(cc, yy, zz):
        return cc * 16 + yy * 8 + zz

    def copy(src, dst, sem, dev):
        return pltpu.make_async_remote_copy(
            src_ref=src, dst_ref=dst, send_sem=send.at[sem], recv_sem=recv.at[sem],
            device_id=dev, device_id_type=MESH)

    def spectrum_copy(at_slot, sem, dev):
        return copy(g.at[at_slot], g.at[at_slot], sem, dev)

    barrier = pltpu.get_barrier_semaphore()
    greeted = [up[d] for d in ORDER[:-1]] + peers[1:] + [across, sibling]
    for dev in greeted:
        pl.semaphore_signal(barrier, inc=1, device_id=dev, device_id_type=MESH)
    loads = [pltpu.make_async_copy(a, b, local.at[n]) for n, (a, b) in enumerate(
        ((y_h.at[0, 0], y), (dr_h, dr), (dc_h, dc), (ext_h, ext),
         (frames.at[:, 0], x.at[:, 16:528, B:1152]), (ey_h, ey), (ex_h, ex)))]
    for cp in loads:
        cp.start()
    x[:, 0:16, :] = jnp.zeros((2, 16, 1280), BF)
    x[:, 528:544, :] = jnp.zeros((2, 16, 1280), BF)
    x[:, 16:528, 0:B] = jnp.zeros((2, 512, B), BF)
    x[:, 16:528, 1152:1280] = jnp.zeros((2, 512, B), BF)
    r64[...] = jnp.zeros_like(r64)
    for cp in loads[:3]:
        cp.wait()
    mine = slot(c, yh, z)
    main, nyq = own_spectrum(y[...], dr[...], dc[...])
    g[mine, 0:B, :] = main
    g[mine, B : B + 16, :] = nyq
    pl.semaphore_wait(barrier, len(greeted))
    for d in NEAR:
        spectrum_copy(mine, GZ + d, up[d]).start()
    spectrum_copy(mine, GY, across).start()
    spectrum_copy(mine, GS, sibling).start()
    loads[3].wait()
    stage_tables(ext, extc, extr)
    for cp in loads[4:]:
        cp.wait()

    def z_arrived(d):
        s = slot(c, yh, (z + 8 - d) % 8)
        spectrum_copy(s, GZ + d, up[d]).wait_recv()
        spectrum_copy(s, GY + d, across).start()
        spectrum_copy(s, GS + d, sibling).start()

    def y_arrived(d):
        s = slot(c, 1 - yh, (z + 8 - d) % 8)
        spectrum_copy(s, GY + d, across).wait_recv()
        spectrum_copy(s, GS + 8 + d, sibling).start()

    def sibling_arrived(k):
        for d in range(8):
            s = slot(1 - c, yh if k == 0 else 1 - yh, (z + 8 - d) % 8)
            spectrum_copy(s, GS + 8 * k + d, sibling).wait_recv()

    def sum_a(n):
        return copy(part.at[pl.ds(8 * n, 8)], ra.at[pl.ds(8 * n, 8)], SA + n, sibling)

    def sum_z(d):
        return copy(sc.at[ORDER.index(d)], rc.at[d - 1], SZ + d, up[d])

    def sum_y():
        return copy(sb, rb, SY, across)

    def pair(d):
        n = ORDER.index(d)
        here, there = part[16 + 2 * n : 18 + 2 * n], ra[2 * n : 2 * n + 2]
        return here.astype(F32) + there.astype(F32)

    def send_z(ds):
        for d in ds:
            sc[ORDER.index(d)] = pair(d).astype(BF)
            sum_z(d).start()

    def slot_of(w):
        cc = jnp.where(w < 16, 1 - c, c)
        m = (w % 16) // 4
        d = jnp.where((w // 2) % 2 == 0, 4 + m, 3 - m)
        return cc * 16 + (w % 2) * 8 + (z + d) % 8

    def phase(step, order, **events):
        def group(n, _):
            for j in range(4):
                step((n if order else 7 - n) * 4 + j)
            for name, event in events.items():
                pl.when(n == int(name[1:]))(event)
            return 0

        lax.fori_loop(0, 8, group, 0)

    def z_arrivals(*ds):
        for d in ds:
            z_arrived(d)

    def y_arrivals(*ds):
        for d in ds:
            y_arrived(d)

    def warp_step(w):
        part[w] = warp_block(slot_of(w), codes, x, extc, extr).astype(BF)

    def z_event(*ds):
        return lambda: z_arrivals(*ds)

    def y_event(*ds):
        return lambda: y_arrivals(*ds)

    def chain(*events):
        def run():
            for event in events:
                event()
        return run

    def send_a(n):
        return lambda: sum_a(n).start()

    def z_sums(*ds):
        return lambda: send_z(ds)

    def await_a(n):
        return lambda: sum_a(n).wait_recv()

    phase(warp_step, True, **WARP_EVENTS(chain, z_event, y_event, send_a, await_a, z_sums))

    def front_step(w):
        front(slot_of(w), x, dr[...], dc[...], r64, cr, ci)

    phase(front_step, True, **FRONT_EVENTS(chain, z_event, y_event, send_a, await_a, z_sums))

    def window_copy(d):
        return copy(sent.at[d], rp.at[d - 1], CP + d, peers[d])

    def correlate(cc, last):
        def middle_group(n, _):
            if last:
                pl.when(n == 0)(lambda: sibling_arrived(0))
                pl.when(n == 2)(lambda: sibling_arrived(1))
            for j in range(4):
                middle(slot(cc, jnp.where(n < 2, yh, 1 - yh), (n % 2) * 4 + j), g, cr, ci, mg, sums)
            return 0

        lax.fori_loop(0, 4, middle_group, 0)
        nyquist(cc, g, r64, dc[...], ey[...], sums, mean, q64)

        def back_groups(h, _):
            for e in range(4):
                n = 4 * h + e
                zt = (p + 1 + n) % 8
                for yy in range(2):
                    back(cc, yy, zt, n, 2 * e + yy, codes, cr, ci, mg, mean, q64, ey[...], ex[...], win, flat)
                if last:
                    sent[(n + 1) % 8] = flatten(flat, n)
            if last:
                for d in range(1, 8):
                    pl.when(h == (d - 1) // 4)(lambda d=d: window_copy(d).start())
            return 0

        lax.fori_loop(0, 2, back_groups, 0)

    correlate(c, False)
    correlate(1 - c, True)
    for d in range(1, 8):
        sum_z(d).wait_recv()

    def summed(yy):
        total = part[30 + yy].astype(F32) + ra[14 + yy].astype(F32)
        for d in range(7):
            total = total + rc[d, yy].astype(F32)
        return total

    sb[...] = summed(1 - yh).astype(BF)
    sum_y().start()
    own[...] = summed(yh)
    for d in range(8):
        if d:
            spectrum_copy(mine, GZ + d, up[d]).wait_send()
            sum_z(d).wait_send()
        spectrum_copy(mine, GY + d, across).wait_send()
        spectrum_copy(mine, GS + d, sibling).wait_send()
        spectrum_copy(mine, GS + 8 + d, sibling).wait_send()
    sum_a(0).wait_send()
    sum_a(1).wait_send()
    for d in range(1, 8):
        window_copy(d).wait_recv()
    total = sent[0]
    for d in range(7):
        total = total + rp[d]
    out_c[0] = total[0:4]
    out_c[1] = total[4:8]
    sum_y().wait_recv()
    out_t[0, 0] = (own[...] + rb[...].astype(F32)) * (1.0 / 64)
    sum_y().wait_send()
    for d in range(1, 8):
        window_copy(d).wait_send()


def on_device(frames, template, codes):
    vm = pltpu.VMEM
    dma = pltpu.SemaphoreType.DMA
    return pl.pallas_call(
        kernel,
        out_shape=[jax.ShapeDtypeStruct((2, 4, 256), F32), jax.ShapeDtypeStruct((1, 1, B, B), F32)],
        in_specs=[SM] + [ANY] * 7,
        out_specs=[VM, VM],
        scratch_shapes=[
            vm((2, 544, 1280), BF), vm((16, 336, B), BF), vm((16, 272, B), F32), vm((32, 144, B), F32),
            vm((B, B), BF), vm((2 * B, 2 * B), BF), vm((2 * B, 2 * B), BF), vm((64, 2 * B), BF), vm((2 * B, B), BF),
            vm((NB, 144, B), BF), vm((B, B), F32),
            vm((NB, B, B), F32), vm((NB, B, B), F32), vm((NB, B, B), F32),
            vm((NB, B), F32), vm((NB, B), F32), vm((32, B), F32),
            vm((8, 32, B), F32), vm((8 * B, B), F32), vm((8, 8, 2 * B), F32),
            vm((NB, B, B), BF), vm((16, B, B), BF), vm((B, B), BF), vm((B, B), BF),
            vm((8, 2, B, B), BF), vm((7, 2, B, B), BF), vm((7, 8, 2 * B), F32), vm((B, B), F32),
            dma((7,)), dma((NSEM,)), dma((NSEM,)),
        ],
        compiler_params=pltpu.CompilerParams(
            collective_id=0, has_side_effects=True, vmem_limit_bytes=67043328),
    )(codes, frames, template, *tables())


def solution(mesh):
    in_specs = (P("tm", "plane", None, None), P("tm", "plane", None, None), P("tm", None, None))
    out_specs = (P("tm", "plane", None), P("tm", "plane", None, None))
    return jax.shard_map(on_device, mesh=mesh, in_specs=in_specs, out_specs=out_specs, check_vma=False)
```
